32 devices in a mesh: groups: 2 (over y), row: 8 (over z, x), section: 2 (over core).
Axes of the slice: x: 2, y: 2, z: 4, core: 2. Of those that a mesh axis runs over, the one named last changes fastest.
Arguments:
- hidden: bfloat16 [64, 8192], P('groups', ('row', 'section')), parts along dimension 0, may hold values from -6 to 6
- norm_in_gain: float32 [8192], replicated, may hold values from 0.1 to 1.9
- zx_weight: bfloat16 [8192, 2, 8, 64], P(None, None, 'row', 'section'), may hold values from -0.0625 to 0.0625
- bc_weight: bfloat16 [8192, 2048], P(None, ('row', 'section')), may hold values from -0.0625 to 0.0625
- dt_weight: bfloat16 [8192, 8], P(None, 'row'), may hold values from -0.0625 to 0.0625
- dt_bias: float32 [8], P('row'), may hold values from -3 to -0.5
- decay_log: float32 [8], P('row'), may hold values from -0.7 to 2
- skip_gain: float32 [8], P('row'), may hold values from 0.5 to 1.5
- conv_x_weight: float32 [4, 8, 64], P(None, 'row', 'section'), may hold values from -3.6 to 3.6
- conv_x_bias: float32 [8, 64], P('row', 'section'), may hold values from -3 to 3
- conv_bc_weight: float32 [4, 2048], P(None, ('row', 'section')), may hold values from -3 to 3
- conv_bc_bias: float32 [2048], P(('row', 'section')), may hold values from -3 to 3
- conv_x_state: bfloat16 [64, 3, 8, 64], P('groups', None, 'row', 'section'), parts along dimension 0, may hold values from -6 to 6
- conv_bc_state: bfloat16 [64, 3, 2048], P('groups', None, ('row', 'section')), parts along dimension 0, may hold values from -6 to 6
- ssm_state: bfloat16 [64, 8, 64, 256], P('groups', 'row', 'section'), parts along dimension 0, may hold values from -6 to 6
- gate_norm_weight: float32 [8, 64], P('row', 'section'), may hold values from 0.1 to 1.9
- out_weight: bfloat16 [8, 64, 8192], P('row', 'section'), may hold values from -0.375 to 0.375
- norm_mid_gain: float32 [8192], replicated, may hold values from 0.1 to 1.9
- up_weight: bfloat16 [8192, 16384], P(None, ('row', 'section')), may hold values from -0.0625 to 0.0625
- down_weight: bfloat16 [16384, 8192], P(('row', 'section')), may hold values from -0.0625 to 0.0625
- valid: int32 [64], P('groups'), parts along dimension 0, may hold values 0 or 1
Outputs:
- block_out: bfloat16 [64, 8192], P('groups', ('row', 'section')), parts along dimension 0
- new_ssm_state: bfloat16 [64, 8, 64, 256], P('groups', 'row', 'section'), parts along dimension 0
- new_conv_x_state: bfloat16 [64, 3, 8, 64], P('groups', None, 'row', 'section'), parts along dimension 0
- new_conv_bc_state: bfloat16 [64, 3, 2048], P('groups', None, ('row', 'section')), parts along dimension 0
The draws below stay inside these ranges and needn't reach their ends.
There are 2 independent parts, one for each index of `groups`. The reference program is written for one: setup_inputs(seed, part) draws one part's arguments, and reference() takes and returns one part's arrays. A program takes and returns all parts, laid end to end along the dimension named above; an argument that names none is the same for every part. Nothing has to cross between parts.
All inputs are finite; a program needn't handle non-finite values.
Results may differ from the reference program's by a relative error of at most 0.0075.
Values may be sent and summed in bfloat16 or wider, within the bound.
A program may use at most 128 MiB of HBM per device.

```python
import jax
import jax.numpy as jnp
from jax import lax

D = 8192
FF = 16384
HEAD_DIM = 64
STATE = 256
GROUPS = 4
ROWS = 32
HEADS = 8
BCW = 2048


def draw_conv_x_weight(key, part):
    base = jnp.clip(jax.random.normal(key, (4, HEADS, HEAD_DIM), jnp.float32), -2.0, 2.0) * 0.75
    channel = jnp.arange(HEADS, dtype=jnp.float32)[:, None] * HEAD_DIM + jnp.arange(HEAD_DIM, dtype=jnp.float32)[None, :]
    factor = 0.6 + 1.2 * channel / (HEADS * HEAD_DIM - 1)
    return base * factor[None]


def place_ends(drawn, own_key, least, high):
    index_at = [jax.random.randint(jax.random.fold_in(own_key, axis), (), 0, length) for axis, length in enumerate(drawn.shape)]
    main_axis = drawn.shape.index(max(drawn.shape))
    next_to = index_at[:main_axis] + [(index_at[main_axis] + 1) % drawn.shape[main_axis]] + index_at[main_axis + 1:]
    return drawn.at[tuple(index_at)].set(least).at[tuple(next_to)].set(high)


def strengthened(entries, key, source, target, blocks, factor):
    def block_of(axis_at):
        return (jnp.arange(entries.shape[axis_at]) // (entries.shape[axis_at] // blocks)).reshape((-1,) + (1,) * (entries.ndim - 1 - axis_at))

    first = jax.random.permutation(key, blocks)[block_of(target)]
    far = (block_of(target) + blocks // 2) % blocks
    return jnp.where((block_of(source) == first) | (block_of(source) == far), factor * entries, entries)


def block_scale(stream_key, shape, split, least, top_value):
    level = 1.0
    for dim, blocks in split:
        heights = jax.random.uniform(jax.random.fold_in(jax.random.fold_in(stream_key, 6), dim), (blocks,), jnp.float32, least / len(split), top_value / len(split))
        level = level * jnp.repeat(jnp.exp(heights), shape[dim] // blocks).reshape((-1,) + (1,) * (len(shape) - 1 - dim))
    return level


def gaussian(own_key, extent, width, most, pieces=(), held_as=jnp.bfloat16):
    values = jax.random.normal(own_key, extent, jnp.float32) * width
    if len(pieces) > 0:
        values = block_scale(own_key, extent, pieces, -0.22, 0.18) * values
    return jnp.clip(values, min=-most, max=most).astype(held_as)


def heavy_noise(own_key, extent, width, limit, cuts, heavy, kind=jnp.bfloat16):
    result = width * jax.random.normal(own_key, extent, jnp.float32)
    if cuts:
        result = result * block_scale(own_key, extent, cuts, -0.22, 0.18)
    return jnp.clip(strengthened(result, jax.random.fold_in(own_key, 3), *heavy), -limit, limit).astype(kind)


def setup_inputs(seed: int = 0, part: int = 0) -> dict:
    arg_keys = jax.random.split(jax.random.key(seed), 22)
    part_keys = jax.random.split(jax.random.fold_in(arg_keys[21], part), 22)
    hidden = gaussian(part_keys[0], (ROWS, D), 1.0, 6.0, ((1, 16),))
    norm_in_gain = jnp.clip(1.0 + 0.18 * jax.random.normal(arg_keys[1], (D,), jnp.float32), 0.1, 1.9)
    zx_weight = gaussian(arg_keys[2], (D, 2, HEADS, HEAD_DIM), D ** -0.5, 0.0625, ((2, 8), (3, 2)))
    bc_weight = gaussian(arg_keys[3], (D, BCW), D ** -0.5, 0.0625, ((1, 16),))
    dt_weight = gaussian(arg_keys[4], (D, HEADS), D ** -0.5, 0.0625, ((1, 8),))
    dt_bias = jnp.clip(-3.0 + 2.5 * jax.random.uniform(arg_keys[5], (HEADS,), jnp.float32) ** block_scale(arg_keys[5], (HEADS,), ((0, 8),), -0.2, 0.2), -3.0, -0.5)
    decay_log = jnp.clip(-0.7 + 2.7 * jax.random.uniform(arg_keys[6], (HEADS,), jnp.float32) ** block_scale(arg_keys[6], (HEADS,), ((0, 8),), -0.2, 0.2), -0.7, 2.0)
    skip_gain = jnp.clip(0.5 + 1.0 * jax.random.uniform(arg_keys[7], (HEADS,), jnp.float32) ** block_scale(arg_keys[7], (HEADS,), ((0, 8),), -0.2, 0.2), 0.5, 1.5)
    conv_x_weight = draw_conv_x_weight(jax.random.fold_in(arg_keys[21], 71), part)
    conv_x_bias = gaussian(arg_keys[9], (HEADS, HEAD_DIM), 0.5, 3.0, ((0, 8), (1, 2)), jnp.float32)
    conv_bc_weight = gaussian(arg_keys[10], (4, BCW), 4 ** -0.5, 3.0, ((1, 16),), jnp.float32)
    conv_bc_bias = gaussian(arg_keys[11], (BCW,), 0.5, 3.0, ((0, 16),), jnp.float32)
    conv_x_state = gaussian(part_keys[12], (ROWS, 3, HEADS, HEAD_DIM), 1.0, 6.0, ((2, 8), (3, 2)))
    conv_bc_state = gaussian(part_keys[13], (ROWS, 3, BCW), 1.0, 6.0, ((2, 16),))
    ssm_state = gaussian(part_keys[14], (ROWS, HEADS, HEAD_DIM, STATE), 1.0, 6.0, ((1, 8), (2, 2)))
    gate_norm_weight = jnp.clip(1.0 + 0.18 * jax.random.normal(arg_keys[15], (HEADS, HEAD_DIM), jnp.float32), 0.1, 1.9)
    out_weight = heavy_noise(arg_keys[16], (HEADS, HEAD_DIM, D), (HEADS * HEAD_DIM) ** -0.5, 0.375, ((0, 8), (1, 2)), (0, 2, 8, 2.0))
    norm_mid_gain = jnp.clip(1.0 + 0.18 * jax.random.normal(arg_keys[17], (D,), jnp.float32), 0.1, 1.9)
    up_weight = gaussian(arg_keys[18], (D, FF), D ** -0.5, 0.0625, ((1, 16),))
    down_weight = heavy_noise(arg_keys[19], (FF, D), FF ** -0.5, 0.0625, ((0, 16),), (0, 1, 16, 2.0))
    valid = place_ends((jax.random.randint(part_keys[20], (ROWS,), 0, 4) < 3).astype(jnp.int32), jax.random.fold_in(part_keys[20], 1), 0, 1)
    return dict(hidden=hidden, norm_in_gain=norm_in_gain, zx_weight=zx_weight, bc_weight=bc_weight, dt_weight=dt_weight, dt_bias=dt_bias, decay_log=decay_log, skip_gain=skip_gain, conv_x_weight=conv_x_weight, conv_x_bias=conv_x_bias, conv_bc_weight=conv_bc_weight, conv_bc_bias=conv_bc_bias, conv_x_state=conv_x_state, conv_bc_state=conv_bc_state, ssm_state=ssm_state, gate_norm_weight=gate_norm_weight, out_weight=out_weight, norm_mid_gain=norm_mid_gain, up_weight=up_weight, down_weight=down_weight, valid=valid)


def mean_norm(values, gain):
    return values * lax.rsqrt(lax.optimization_barrier(jnp.mean(values * values, axis=-1, keepdims=True)) + 1e-05) * gain

def reference(hidden, norm_in_gain, zx_weight, bc_weight, dt_weight, dt_bias, decay_log, skip_gain, conv_x_weight, conv_x_bias, conv_bc_weight, conv_bc_bias, conv_x_state, conv_bc_state, ssm_state, gate_norm_weight, out_weight, norm_mid_gain, up_weight, down_weight, valid):
    row_count = hidden.shape[0]
    channels = HEADS * HEAD_DIM
    full_rows = hidden.astype(jnp.float32)
    normed = mean_norm(full_rows, norm_in_gain.astype(jnp.float32)).astype(jnp.bfloat16)
    gate_inner = jnp.dot(normed, zx_weight.reshape(D, 2 * channels), preferred_element_type=jnp.float32).reshape(row_count, 2, HEADS, HEAD_DIM)
    gate_part = gate_inner[:, 0]
    inner_pre = gate_inner[:, 1].astype(jnp.bfloat16)
    bc_pre = jnp.dot(normed, bc_weight, preferred_element_type=jnp.float32).astype(jnp.bfloat16)
    dt_raw = jnp.dot(normed, dt_weight, preferred_element_type=jnp.float32)
    taps_x = jnp.concatenate([conv_x_state, inner_pre[:, None]], axis=1)
    inner = jax.nn.silu(lax.optimization_barrier(jnp.sum(taps_x.astype(jnp.float32) * conv_x_weight.astype(jnp.float32)[None], axis=1)) + conv_x_bias.astype(jnp.float32))
    taps_bc = jnp.concatenate([conv_bc_state, bc_pre[:, None]], axis=1)
    mixed_bc = jax.nn.silu(lax.optimization_barrier(jnp.sum(taps_bc.astype(jnp.float32) * conv_bc_weight.astype(jnp.float32)[None], axis=1)) + conv_bc_bias.astype(jnp.float32))
    state_in = mixed_bc[:, :GROUPS * STATE].reshape(row_count, GROUPS, STATE)
    state_out = mixed_bc[:, GROUPS * STATE:].reshape(row_count, GROUPS, STATE)
    per_group = HEADS // GROUPS
    in_heads = jnp.repeat(state_in, per_group, axis=1)
    out_heads = jnp.repeat(state_out, per_group, axis=1)
    step_size = jax.nn.softplus(dt_raw + dt_bias.astype(jnp.float32)[None])
    decay_rate = jnp.exp(-step_size * jnp.exp(decay_log.astype(jnp.float32))[None])
    previous = ssm_state.astype(jnp.float32)
    updated = decay_rate[:, :, None, None] * previous + (step_size[:, :, None] * inner)[..., None] * in_heads[:, :, None, :]
    readout = jnp.einsum('rhpn,rhn->rhp', updated, out_heads, precision=lax.Precision.HIGHEST) + skip_gain.astype(jnp.float32)[None, :, None] * inner
    gated = readout * jax.nn.silu(gate_part)
    grouped = gated.reshape(row_count, GROUPS, per_group * HEAD_DIM)
    group_mean = lax.optimization_barrier(jnp.mean(grouped * grouped, axis=-1))
    head_mean = jnp.repeat(group_mean, per_group, axis=1)
    scaled = (gated * lax.rsqrt(head_mean + 1e-05)[:, :, None] * gate_norm_weight.astype(jnp.float32)[None]).astype(jnp.bfloat16)
    mixer = jnp.dot(scaled.reshape(row_count, channels), out_weight.reshape(channels, D), preferred_element_type=jnp.float32)
    middle = (full_rows + mixer).astype(jnp.bfloat16)
    mlp_in = mean_norm(middle.astype(jnp.float32), norm_mid_gain.astype(jnp.float32)).astype(jnp.bfloat16)
    up_values = jnp.dot(mlp_in, up_weight, preferred_element_type=jnp.float32)
    activated = jnp.square(jax.nn.relu(up_values)).astype(jnp.bfloat16)
    down_values = jnp.dot(activated, down_weight, preferred_element_type=jnp.float32)
    block_out = (middle.astype(jnp.float32) + down_values).astype(jnp.bfloat16)
    kept_rows = valid != 0
    new_ssm_state = jnp.where(kept_rows[:, None, None, None], updated, previous).astype(jnp.bfloat16)
    new_conv_x_state = jnp.where(kept_rows[:, None, None, None], taps_x[:, 1:], conv_x_state)
    new_conv_bc_state = jnp.where(kept_rows[:, None, None], taps_bc[:, 1:], conv_bc_state)
    return (block_out, new_ssm_state, new_conv_x_state, new_conv_bc_state)
```

```python
import functools

import jax
import jax.numpy as jnp
from jax import lax
from jax.experimental import pallas as pl
from jax.experimental.pallas import tpu as pltpu
from jax.sharding import PartitionSpec as P

D = 8192
HEAD_DIM = 64
STATE = 256
GROUPS = 4


def mean_norm(values, gain):
    return values * lax.rsqrt(jnp.mean(values * values, axis=-1, keepdims=True) + 1e-05) * gain


def body(
    hidden,
    norm_in_gain,
    zx_weight,
    bc_weight,
    dt_weight,
    dt_bias,
    decay_log,
    skip_gain,
    conv_x_weight,
    conv_x_bias,
    conv_bc_weight,
    conv_bc_bias,
    conv_x_state,
    conv_bc_state,
    ssm_state,
    gate_norm_weight,
    out_weight,
    norm_mid_gain,
    up_weight,
    down_weight,
    valid,
):
    row_count = hidden.shape[0]
    local_p = zx_weight.shape[3]
    full_rows = lax.all_gather(hidden, ("row", "section"), axis=1, tiled=True)
    normed = mean_norm(full_rows.astype(jnp.float32), norm_in_gain).astype(jnp.bfloat16)
    gate_inner = jnp.dot(
        normed, zx_weight.reshape(D, 2 * local_p), preferred_element_type=jnp.float32
    ).reshape(row_count, 2, 1, local_p)
    gate_part = gate_inner[:, 0]
    inner_pre = gate_inner[:, 1].astype(jnp.bfloat16)
    bc_pre = jnp.dot(normed, bc_weight, preferred_element_type=jnp.float32).astype(jnp.bfloat16)
    dt_raw = jnp.dot(normed, dt_weight, preferred_element_type=jnp.float32)
    taps_x = jnp.concatenate([conv_x_state, inner_pre[:, None]], axis=1)
    inner = jax.nn.silu(
        jnp.sum(taps_x.astype(jnp.float32) * conv_x_weight[None], axis=1) + conv_x_bias
    )
    taps_bc = jnp.concatenate([conv_bc_state, bc_pre[:, None]], axis=1)
    mixed_bc = jax.nn.silu(
        jnp.sum(taps_bc.astype(jnp.float32) * conv_bc_weight[None], axis=1) + conv_bc_bias
    )
    all_bc = lax.all_gather(mixed_bc, ("row", "section"), axis=1, tiled=True)
    per_group = lax.axis_size("row") // GROUPS
    group_index = lax.axis_index("row") // per_group
    state_in = all_bc[:, : GROUPS * STATE].reshape(row_count, GROUPS, STATE)
    state_out = all_bc[:, GROUPS * STATE :].reshape(row_count, GROUPS, STATE)
    in_mine = lax.dynamic_slice_in_dim(state_in, group_index, 1, axis=1)
    out_mine = lax.dynamic_slice_in_dim(state_out, group_index, 1, axis=1)
    step_size = jax.nn.softplus(dt_raw + dt_bias[None])
    decay_rate = jnp.exp(-step_size * jnp.exp(decay_log)[None])
    previous = ssm_state.astype(jnp.float32)
    updated = (
        decay_rate[:, :, None, None] * previous
        + (step_size[:, :, None] * inner)[..., None] * in_mine[:, :, None, :]
    )
    readout = (
        jnp.einsum("rhpn,rhn->rhp", updated, out_mine, precision=lax.Precision.HIGHEST)
        + skip_gain[None, :, None] * inner
    )
    gated = readout * jax.nn.silu(gate_part)
    local_squares = jnp.sum(gated * gated, axis=(1, 2))
    group_pick = (jnp.arange(GROUPS) == group_index).astype(jnp.float32)
    group_sums = lax.psum(local_squares[:, None] * group_pick[None], ("row", "section"))
    group_size = per_group * HEAD_DIM
    group_mean = jnp.sum(group_sums * group_pick[None], axis=1) / group_size
    scaled = (gated * lax.rsqrt(group_mean + 1e-05)[:, None, None] * gate_norm_weight[None]).astype(
        jnp.bfloat16
    )
    mixer_terms = jnp.dot(
        scaled.reshape(row_count, local_p),
        out_weight.reshape(local_p, D),
        preferred_element_type=jnp.float32,
    )
    mixer_share = lax.psum_scatter(mixer_terms, ("row", "section"), scatter_dimension=1, tiled=True)
    middle = (hidden.astype(jnp.float32) + mixer_share).astype(jnp.bfloat16)
    middle_full = lax.all_gather(middle, ("row", "section"), axis=1, tiled=True)
    mlp_in = mean_norm(middle_full.astype(jnp.float32), norm_mid_gain).astype(jnp.bfloat16)
    up_values = jnp.dot(mlp_in, up_weight, preferred_element_type=jnp.float32)
    activated = jnp.square(jax.nn.relu(up_values)).astype(jnp.bfloat16)
    down_terms = jnp.dot(activated, down_weight, preferred_element_type=jnp.float32)
    down_share = lax.psum_scatter(down_terms, ("row", "section"), scatter_dimension=1, tiled=True)
    block_out = (middle.astype(jnp.float32) + down_share).astype(jnp.bfloat16)
    kept_rows = valid != 0
    new_ssm_state = jnp.where(kept_rows[:, None, None, None], updated, previous).astype(
        jnp.bfloat16
    )
    new_conv_x_state = jnp.where(kept_rows[:, None, None, None], taps_x[:, 1:], conv_x_state)
    new_conv_bc_state = jnp.where(kept_rows[:, None, None], taps_bc[:, 1:], conv_bc_state)
    return (block_out, new_ssm_state, new_conv_x_state, new_conv_bc_state)


HI = lax.Precision.HIGHEST
MESH = pl.DeviceIdType.MESH
NT = (((1,), (1,)), ((), ()))


def fits(mesh):
    rows, sections = mesh.shape["row"], mesh.shape["section"]
    devices = rows * sections
    return sections == 2 and devices == 16 and rows % GROUPS == 0


def silu(values):
    return values / (1.0 + jnp.exp(-values))


def fused_kernel(
    R,
    hid, gin, zxt, bcw, dtt, dtb, dlog, skip, cxw, cxb, cbw, cbb, cxs, cbs, ssm, gnw, outw, gmid,
    upw, dnw, valid,
    out, new_ssm, new_cx, new_cb,
    zx_v, bc_v, ssm_v, up_v, dn_v, hid_all, owt, bc_out, bc_all, g_out, g_all, mid, mid_all,
    act, send_a, recv_a, send_b, recv_b, own_sum,
    w_sem, h_send, h_recv, o_send, o_recv, bc_send, bc_recv, g_send, g_recv, m_send, m_recv,
    a_send, a_recv, b_send, b_recv,
):
    N = 2 * R
    grp, row, sec = lax.axis_index("groups"), lax.axis_index("row"), lax.axis_index("section")
    me = row * 2 + sec
    other = 1 - sec
    rows, wd = hid.shape
    local_p = zxt.shape[0] // 2
    model = upw.shape[0]

    def remote(src, dst, ssem, rsem, r, s):
        return pltpu.make_async_remote_copy(
            src_ref=src, dst_ref=dst, send_sem=ssem, recv_sem=rsem,
            device_id=(grp, r, s), device_id_type=MESH,
        )

    pending = []

    loads = [
        pltpu.make_async_copy(bcw, bc_v, w_sem.at[0]),
        pltpu.make_async_copy(zxt, zx_v, w_sem.at[1]),
        pltpu.make_async_copy(ssm, ssm_v, w_sem.at[2]),
        pltpu.make_async_copy(upw, up_v, w_sem.at[3]),
        pltpu.make_async_copy(dnw, dn_v, w_sem.at[4]),
    ]

    barrier = pltpu.get_barrier_semaphore()
    for k in range(1, N):
        peer = lax.rem(me + k, N)
        pl.semaphore_signal(
            barrier, inc=1, device_id=(grp, peer // 2, peer % 2), device_id_type=MESH
        )
    for copy in loads:
        copy.start()
    hid_all[me] = hid[...]
    pl.semaphore_wait(barrier, N - 1)

    def gather_start(src, buf, ssem, rsem):
        for k in range(1, R):
            copy = remote(src, buf.at[me], ssem.at[k], rsem.at[me], lax.rem(row + k, R), sec)
            copy.start()
            pending.append(copy)
        copy = remote(src, buf.at[me], ssem.at[0], rsem.at[me], row, other)
        copy.start()
        pending.append(copy)

    def gather_finish(buf, ssem, rsem):
        for k in range(1, R):
            blk = lax.rem(row + R - k, R) * 2 + sec
            copy = remote(buf.at[blk], buf.at[blk], ssem.at[R + k - 1], rsem.at[blk], row, other)
            copy.wait_recv()
            copy.start()
            pending.append(copy)
        for k in range(R):
            blk = lax.rem(row + R - k, R) * 2 + other
            remote(buf.at[blk], buf.at[blk], ssem.at[0], rsem.at[blk], row, other).wait_recv()

    gather_start(hid, hid_all, h_send, h_recv)

    eye = (
        lax.broadcasted_iota(jnp.int32, (local_p, local_p), 0)
        == lax.broadcasted_iota(jnp.int32, (local_p, local_p), 1)
    ).astype(jnp.float32)

    def turn(values):
        return lax.dot_general(eye, values, NT, precision=HI, preferred_element_type=jnp.float32)

    f32 = jnp.float32
    valid_row = (valid[...] != 0).astype(f32)
    valid_col = turn(valid_row)
    pre_x = cxb[...] + sum(cxs[t].astype(f32) * cxw[t : t + 1, :] for t in range(3))
    pre_x_t = turn(pre_x)
    tap_t = turn(cxw[3:4, :])
    gnw_t = turn(gnw[...])
    pre_bc = cbb[...] + sum(cbs[t].astype(f32) * cbw[t : t + 1, :] for t in range(3))

    gather_finish(hid_all, h_send, h_recv)

    for k in range(1, N):
        peer = lax.rem(me + k, N)
        copy = remote(
            outw.at[:, pl.ds(pl.multiple_of(peer * wd, wd), wd)],
            owt.at[me], o_send.at[k], o_recv.at[me], peer // 2, peer % 2,
        )
        copy.start()
        pending.append(copy)
    own_w = pltpu.make_async_copy(
        outw.at[:, pl.ds(pl.multiple_of(me * wd, wd), wd)], owt.at[me], w_sem.at[5]
    )
    own_w.start()

    def inverse_norm(buf):
        def step(b, total):
            values = buf[b].astype(f32)
            squares = values * values
            return total + sum(squares[:, i : i + 128] for i in range(0, wd, 128))

        total = lax.fori_loop(0, N, step, jnp.zeros((rows, 128), f32))
        return lax.rsqrt(jnp.sum(total, axis=1, keepdims=True) / model + 1e-05)

    scale = inverse_norm(hid_all)
    loads[0].wait()
    loads[1].wait()

    def project(b, carry):
        acc_bc, acc_zx, acc_dt = carry
        at = pl.ds(pl.multiple_of(b * wd, wd), wd)
        normed = (hid_all[b].astype(f32) * scale * gin[:, at]).astype(jnp.bfloat16)
        acc_bc += jnp.dot(normed, bc_v[at, :], preferred_element_type=f32)
        acc_zx += lax.dot_general(zx_v[:, at], normed, NT, preferred_element_type=f32)
        dt_rows = jnp.broadcast_to(dtt[:, at].astype(f32), (16, wd)).astype(jnp.bfloat16)
        acc_dt += lax.dot_general(dt_rows, normed, NT, preferred_element_type=f32)
        return acc_bc, acc_zx, acc_dt

    acc_bc, acc_zx, acc_dt = lax.fori_loop(
        0, N, project,
        (
            jnp.zeros((rows, bc_v.shape[1]), f32),
            jnp.zeros((2 * local_p, rows), f32),
            jnp.zeros((16, rows), f32),
        ),
    )
    bc_pre = acc_bc.astype(jnp.bfloat16).astype(f32)
    mixed_bc = silu(pre_bc + bc_pre * cbw[3:4, :])
    bc_out[...] = mixed_bc

    cb = bc_v.shape[1]
    parts = STATE // cb
    half = me // (N // 2)
    to_group = lax.rem(me, N // 2) // parts
    slot = half * parts + lax.rem(me, parts)
    per = N // GROUPS
    my_group = me // per
    for i in range(per):
        dest = to_group * per + i

        @pl.when(dest != me)
        def _():
            remote(
                bc_out, bc_all.at[slot], bc_send.at[i], bc_recv.at[slot], dest // 2, dest % 2
            ).start()

        @pl.when(dest == me)
        def _():
            bc_all[slot] = bc_out[...]

    gate_t = silu(acc_zx[:local_p])
    inner_pre_t = acc_zx[local_p:].astype(jnp.bfloat16).astype(f32)
    inner_t = silu(pre_x_t + inner_pre_t * tap_t)
    dt_sum = acc_dt[0:1] + dtb[...]
    step_size = jnp.maximum(dt_sum, 0.0) + jnp.log1p(jnp.exp(-jnp.abs(dt_sum)))
    decay = jnp.exp(-step_size * jnp.exp(dlog[...]))
    driven_t = inner_t * step_size
    keep_x = jnp.broadcast_to(valid_col, (rows, local_p)) > 0.5
    keep_bc = jnp.broadcast_to(valid_col, (rows, cb)) > 0.5
    last_x = turn(inner_pre_t)
    for t in range(3):
        later_x = last_x if t == 2 else cxs[t + 1].astype(f32)
        later_bc = bc_pre if t == 2 else cbs[t + 1].astype(f32)
        new_cx[t] = jnp.where(keep_x, later_x, cxs[t].astype(f32)).astype(jnp.bfloat16)
        new_cb[t] = jnp.where(keep_bc, later_bc, cbs[t].astype(f32)).astype(jnp.bfloat16)
    loads[2].wait()

    for h in range(2):
        for p in range(parts):
            source = h * (N // 2) + my_group * parts + p

            @pl.when(source != me)
            def _():
                remote(
                    bc_out, bc_all.at[h * parts + p], bc_send.at[0], bc_recv.at[h * parts + p],
                    row, other,
                ).wait_recv()

    state_in = jnp.concatenate([bc_all[p] for p in range(parts)], axis=1)
    state_out = jnp.concatenate([bc_all[parts + p] for p in range(parts)], axis=1)

    lane = lax.broadcasted_iota(jnp.int32, (local_p, rows), 1)

    def updated(r):
        previous = ssm_v[r].astype(f32)
        value = decay[0:1, r : r + 1] * previous + driven_t[:, r : r + 1] * state_in[r : r + 1, :]
        return previous, value

    read_t = jnp.zeros((local_p, rows), f32)
    for r in range(rows):
        _, value = updated(r)
        column = jnp.sum(value * state_out[r : r + 1, :], axis=1, keepdims=True)
        read_t = jnp.where(lane == r, column, read_t)
    gated_t = (read_t + skip[...] * inner_t) * gate_t
    g_out[:, 0:rows] = gated_t
    g_out[:, rows : rows + 1] = gnw_t
    gather_start(g_out, g_all, g_send, g_recv)
    g_all[me] = g_out[...]

    for r in range(rows):
        previous, value = updated(r)
        keep = jnp.broadcast_to(valid_row[0:1, r : r + 1], value.shape) > 0.5
        new_ssm[r] = jnp.where(keep, value, previous).astype(jnp.bfloat16)

    for k in range(1, N):
        peer = lax.rem(me + N - k, N)
        remote(owt.at[peer], owt.at[peer], o_send.at[0], o_recv.at[peer], row, other).wait_recv()
    own_w.wait()
    gather_finish(g_all, g_send, g_recv)

    eye_rows = (
        lax.broadcasted_iota(jnp.int32, (rows, rows), 0)
        == lax.broadcasted_iota(jnp.int32, (rows, rows), 1)
    ).astype(jnp.bfloat16)
    mixed = hid[...].astype(f32)
    for q in range(GROUPS):
        pieces = [g_all[q * per + i, :, 0:rows] for i in range(per)]
        squares = sum(jnp.sum(piece * piece, axis=0, keepdims=True) for piece in pieces)
        norm = lax.rsqrt(squares / (per * local_p) + 1e-05)
        scaled_t = jnp.concatenate(
            [pieces[i] * norm * g_all[q * per + i, :, rows : rows + 1] for i in range(per)], axis=0
        ).astype(jnp.bfloat16)
        scaled = lax.dot_general(eye_rows, scaled_t, NT, preferred_element_type=f32)
        weights = owt[q * per : (q + 1) * per].reshape(per * local_p, wd)
        mixed += jnp.dot(scaled.astype(jnp.bfloat16), weights, preferred_element_type=f32)
    mid[...] = mixed.astype(jnp.bfloat16)
    gather_start(mid, mid_all, m_send, m_recv)
    mid_all[me] = mid[...]
    gather_finish(mid_all, m_send, m_recv)

    scale_mid = inverse_norm(mid_all)
    loads[3].wait()
    ff = up_v.shape[1]
    act[...] = jnp.zeros_like(act)

    def up_step(b, _):
        at = pl.ds(pl.multiple_of(b * wd, wd), wd)
        fed = (mid_all[b].astype(f32) * scale_mid * gmid[:, at]).astype(jnp.bfloat16)
        act[...] += jnp.dot(fed, up_v[at, :], preferred_element_type=f32)
        return 0

    lax.fori_loop(0, N, up_step, 0)
    activated = jnp.square(jnp.maximum(act[...], 0.0)).astype(jnp.bfloat16)
    loads[4].wait()

    def down(block):
        at = pl.ds(pl.multiple_of(block * wd, wd), wd)
        return jnp.dot(activated, dn_v[:, at], preferred_element_type=f32)

    def for_partner(k, _):
        target = lax.rem(row + 1 + k, R)
        send_a[k] = down(target * 2 + other).astype(jnp.bfloat16)
        remote(send_a.at[k], recv_a.at[k], a_send.at[k], a_recv.at[k], row, other).start()
        return 0

    lax.fori_loop(0, R, for_partner, 0)

    def for_chip(k, _):
        target = lax.rem(row + 1 + k, R)
        part = down(target * 2 + sec)
        remote(send_a.at[k], recv_a.at[k], a_send.at[k], a_recv.at[k], row, other).wait()
        send_b[k] = (part + recv_a[k].astype(f32)).astype(jnp.bfloat16)
        remote(send_b.at[k], recv_b.at[row], b_send.at[k], b_recv.at[row], target, sec).start()
        return 0

    lax.fori_loop(0, R - 1, for_chip, 0)
    total = down(me)
    remote(
        send_a.at[R - 1], recv_a.at[R - 1], a_send.at[R - 1], a_recv.at[R - 1], row, other
    ).wait()
    own_sum[...] = total + recv_a[R - 1].astype(f32) + mid[...].astype(f32)

    def collect(k, _):
        source = lax.rem(row + R - 1 - k, R)
        remote(
            send_b.at[k], recv_b.at[source], b_send.at[k], b_recv.at[source], source, sec
        ).wait_recv()
        own_sum[...] += recv_b[source].astype(f32)
        return 0

    lax.fori_loop(0, R - 1, collect, 0)
    out[...] = own_sum[...].astype(jnp.bfloat16)

    def drain(k, _):
        remote(
            send_b.at[k], recv_b.at[row], b_send.at[k], b_recv.at[row], row, other
        ).wait_send()
        return 0

    lax.fori_loop(0, R - 1, drain, 0)
    for i in range(per):
        dest = to_group * per + i

        @pl.when(dest != me)
        def _():
            remote(
                bc_out, bc_all.at[slot], bc_send.at[i], bc_recv.at[slot], row, other
            ).wait_send()

    for copy in pending:
        copy.wait_send()


def fused_body(
    hidden, norm_in_gain, zx_weight, bc_weight, dt_weight, dt_bias, decay_log, skip_gain,
    conv_x_weight, conv_x_bias, conv_bc_weight, conv_bc_bias, conv_x_state, conv_bc_state,
    ssm_state, gate_norm_weight, out_weight, norm_mid_gain, up_weight, down_weight, valid,
):
    R = lax.axis_size("row")
    N = 2 * R
    rows, wd = hidden.shape
    model = up_weight.shape[0]
    p = zx_weight.shape[3]
    cb = bc_weight.shape[1]
    ff = up_weight.shape[1]
    bf16, f32 = jnp.bfloat16, jnp.float32
    vm, hbm = pl.BlockSpec(memory_space=pltpu.VMEM), pl.BlockSpec(memory_space=pl.ANY)
    dma = pltpu.SemaphoreType.DMA
    out, new_ssm, new_cx, new_cb = pl.pallas_call(
        functools.partial(fused_kernel, R),
        out_shape=(
            jax.ShapeDtypeStruct((rows, wd), bf16),
            jax.ShapeDtypeStruct((rows, p, STATE), bf16),
            jax.ShapeDtypeStruct((3, rows, p), bf16),
            jax.ShapeDtypeStruct((3, rows, cb), bf16),
        ),
        in_specs=[
            vm, vm, hbm, hbm, vm, vm, vm, vm, vm, vm, vm, vm, vm, vm, hbm, vm, hbm, vm, hbm, hbm, vm
        ],
        out_specs=(vm, vm, vm, vm),
        scratch_shapes=[
            pltpu.VMEM((2 * p, model), bf16),
            pltpu.VMEM((model, cb), bf16),
            pltpu.VMEM((rows, p, STATE), bf16),
            pltpu.VMEM((model, ff), bf16),
            pltpu.VMEM((ff, model), bf16),
            pltpu.VMEM((N, rows, wd), bf16),
            pltpu.VMEM((N, p, wd), bf16),
            pltpu.VMEM((rows, cb), f32),
            pltpu.VMEM((2 * STATE // cb, rows, cb), f32),
            pltpu.VMEM((p, 128), f32),
            pltpu.VMEM((N, p, 128), f32),
            pltpu.VMEM((rows, wd), bf16),
            pltpu.VMEM((N, rows, wd), bf16),
            pltpu.VMEM((rows, ff), f32),
            pltpu.VMEM((R, rows, wd), bf16),
            pltpu.VMEM((R, rows, wd), bf16),
            pltpu.VMEM((R, rows, wd), bf16),
            pltpu.VMEM((R, rows, wd), bf16),
            pltpu.VMEM((rows, wd), f32),
            dma((6,)), dma((N,)), dma((N,)), dma((N,)), dma((N,)),
            dma((N // GROUPS,)), dma((2 * STATE // cb,)),
            dma((N,)), dma((N,)), dma((N,)), dma((N,)),
            dma((R,)), dma((R,)), dma((R,)), dma((R,)),
        ],
        compiler_params=pltpu.CompilerParams(
            collective_id=0, has_side_effects=True, vmem_limit_bytes=60 * 1024 * 1024
        ),
    )(
        hidden,
        norm_in_gain.reshape(1, model),
        jnp.transpose(zx_weight, (1, 2, 3, 0)).reshape(2 * p, model),
        bc_weight,
        dt_weight.reshape(1, model),
        dt_bias.reshape(1, 1),
        decay_log.reshape(1, 1),
        skip_gain.reshape(1, 1),
        conv_x_weight.reshape(4, p),
        conv_x_bias.reshape(1, p),
        conv_bc_weight,
        conv_bc_bias.reshape(1, cb),
        jnp.transpose(conv_x_state, (1, 2, 0, 3)).reshape(3, rows, p),
        jnp.transpose(conv_bc_state, (1, 0, 2)),
        ssm_state.reshape(rows, p, STATE),
        gate_norm_weight.reshape(1, p),
        out_weight.reshape(p, model),
        norm_mid_gain.reshape(1, model),
        up_weight,
        down_weight,
        valid.reshape(1, rows),
    )
    return (
        out,
        new_ssm.reshape(rows, 1, p, STATE),
        jnp.transpose(new_cx, (1, 0, 2)).reshape(rows, 3, 1, p),
        jnp.transpose(new_cb, (1, 0, 2)),
    )


def solution(mesh):
    chosen = fused_body if fits(mesh) else body
    return jax.shard_map(
        chosen,
        mesh=mesh,
        in_specs=(
            P("groups", ("row", "section")),
            P(),
            P(None, None, "row", "section"),
            P(None, ("row", "section")),
            P(None, "row"),
            P("row"),
            P("row"),
            P("row"),
            P(None, "row", "section"),
            P("row", "section"),
            P(None, ("row", "section")),
            P(("row", "section")),
            P("groups", None, "row", "section"),
            P("groups", None, ("row", "section")),
            P("groups", "row", "section", None),
            P("row", "section"),
            P("row", "section", None),
            P(),
            P(None, ("row", "section")),
            P(("row", "section"), None),
            P("groups"),
        ),
        out_specs=(
            P("groups", ("row", "section")),
            P("groups", "row", "section", None),
            P("groups", None, "row", "section"),
            P("groups", None, ("row", "section")),
        ),
        check_vma=False,
    )
```

```python
import functools

import jax
import jax.numpy as jnp
from jax import lax
from jax.experimental import pallas as pl
from jax.experimental.pallas import tpu as pltpu
from jax.sharding import PartitionSpec as P

D = 8192
HEAD_DIM = 64
STATE = 256
GROUPS = 4


def mean_norm(values, gain):
    return values * lax.rsqrt(jnp.mean(values * values, axis=-1, keepdims=True) + 1e-05) * gain


def body(
    hidden,
    norm_in_gain,
    zx_weight,
    bc_weight,
    dt_weight,
    dt_bias,
    decay_log,
    skip_gain,
    conv_x_weight,
    conv_x_bias,
    conv_bc_weight,
    conv_bc_bias,
    conv_x_state,
    conv_bc_state,
    ssm_state,
    gate_norm_weight,
    out_weight,
    norm_mid_gain,
    up_weight,
    down_weight,
    valid,
):
    row_count = hidden.shape[0]
    local_p = zx_weight.shape[3]
    full_rows = lax.all_gather(hidden, ("row", "section"), axis=1, tiled=True)
    normed = mean_norm(full_rows.astype(jnp.float32), norm_in_gain).astype(jnp.bfloat16)
    gate_inner = jnp.dot(
        normed, zx_weight.reshape(D, 2 * local_p), preferred_element_type=jnp.float32
    ).reshape(row_count, 2, 1, local_p)
    gate_part = gate_inner[:, 0]
    inner_pre = gate_inner[:, 1].astype(jnp.bfloat16)
    bc_pre = jnp.dot(normed, bc_weight, preferred_element_type=jnp.float32).astype(jnp.bfloat16)
    dt_raw = jnp.dot(normed, dt_weight, preferred_element_type=jnp.float32)
    taps_x = jnp.concatenate([conv_x_state, inner_pre[:, None]], axis=1)
    inner = jax.nn.silu(
        jnp.sum(taps_x.astype(jnp.float32) * conv_x_weight[None], axis=1) + conv_x_bias
    )
    taps_bc = jnp.concatenate([conv_bc_state, bc_pre[:, None]], axis=1)
    mixed_bc = jax.nn.silu(
        jnp.sum(taps_bc.astype(jnp.float32) * conv_bc_weight[None], axis=1) + conv_bc_bias
    )
    all_bc = lax.all_gather(mixed_bc, ("row", "section"), axis=1, tiled=True)
    per_group = lax.axis_size("row") // GROUPS
    group_index = lax.axis_index("row") // per_group
    state_in = all_bc[:, : GROUPS * STATE].reshape(row_count, GROUPS, STATE)
    state_out = all_bc[:, GROUPS * STATE :].reshape(row_count, GROUPS, STATE)
    in_mine = lax.dynamic_slice_in_dim(state_in, group_index, 1, axis=1)
    out_mine = lax.dynamic_slice_in_dim(state_out, group_index, 1, axis=1)
    step_size = jax.nn.softplus(dt_raw + dt_bias[None])
    decay_rate = jnp.exp(-step_size * jnp.exp(decay_log)[None])
    previous = ssm_state.astype(jnp.float32)
    updated = (
        decay_rate[:, :, None, None] * previous
        + (step_size[:, :, None] * inner)[..., None] * in_mine[:, :, None, :]
    )
    readout = (
        jnp.einsum("rhpn,rhn->rhp", updated, out_mine, precision=lax.Precision.HIGHEST)
        + skip_gain[None, :, None] * inner
    )
    gated = readout * jax.nn.silu(gate_part)
    local_squares = jnp.sum(gated * gated, axis=(1, 2))
    group_pick = (jnp.arange(GROUPS) == group_index).astype(jnp.float32)
    group_sums = lax.psum(local_squares[:, None] * group_pick[None], ("row", "section"))
    group_size = per_group * HEAD_DIM
    group_mean = jnp.sum(group_sums * group_pick[None], axis=1) / group_size
    scaled = (gated * lax.rsqrt(group_mean + 1e-05)[:, None, None] * gate_norm_weight[None]).astype(
        jnp.bfloat16
    )
    mixer_terms = jnp.dot(
        scaled.reshape(row_count, local_p),
        out_weight.reshape(local_p, D),
        preferred_element_type=jnp.float32,
    )
    mixer_share = lax.psum_scatter(mixer_terms, ("row", "section"), scatter_dimension=1, tiled=True)
    middle = (hidden.astype(jnp.float32) + mixer_share).astype(jnp.bfloat16)
    middle_full = lax.all_gather(middle, ("row", "section"), axis=1, tiled=True)
    mlp_in = mean_norm(middle_full.astype(jnp.float32), norm_mid_gain).astype(jnp.bfloat16)
    up_values = jnp.dot(mlp_in, up_weight, preferred_element_type=jnp.float32)
    activated = jnp.square(jax.nn.relu(up_values)).astype(jnp.bfloat16)
    down_terms = jnp.dot(activated, down_weight, preferred_element_type=jnp.float32)
    down_share = lax.psum_scatter(down_terms, ("row", "section"), scatter_dimension=1, tiled=True)
    block_out = (middle.astype(jnp.float32) + down_share).astype(jnp.bfloat16)
    kept_rows = valid != 0
    new_ssm_state = jnp.where(kept_rows[:, None, None, None], updated, previous).astype(
        jnp.bfloat16
    )
    new_conv_x_state = jnp.where(kept_rows[:, None, None, None], taps_x[:, 1:], conv_x_state)
    new_conv_bc_state = jnp.where(kept_rows[:, None, None], taps_bc[:, 1:], conv_bc_state)
    return (block_out, new_ssm_state, new_conv_x_state, new_conv_bc_state)


HI = lax.Precision.HIGHEST
MESH = pl.DeviceIdType.MESH
NT = (((1,), (1,)), ((), ()))


def fits(mesh):
    return mesh.shape["section"] == 2 and mesh.shape["row"] == 2 * GROUPS


def silu(values):
    return values / (1.0 + jnp.exp(-values))


def fused_kernel(
    R,
    hid, gin, zxt, bcw, dtt, dtb, dlog, skip, cxw, cxb, cbw, cbb, cxs, cbs, ssm, gnw, outw, gmid,
    upw, dnw, valid,
    out, new_ssm, new_cx, new_cb,
    zx_v, bc_v, ssm_v, up_v, dn_v, hid_all, owt, bc_out, bc_all, g_out, g_all, mid, mid_all,
    send_m, recv_m, act, send_a, recv_a, send_b, recv_b, own_sum,
    w_sem, h_send, h_recv, o_send, o_recv, bc_send, bc_recv, g_send, g_recv, m_send, m_recv,
    a_send, a_recv, b_send, b_recv, x_send, x_recv,
):
    N = 2 * R
    grp, row, sec = lax.axis_index("groups"), lax.axis_index("row"), lax.axis_index("section")
    me = row * 2 + sec
    other = 1 - sec
    rows, wd = hid.shape
    local_p = zxt.shape[0] // 2
    model = upw.shape[0]

    def remote(src, dst, ssem, rsem, r, s):
        return pltpu.make_async_remote_copy(
            src_ref=src, dst_ref=dst, send_sem=ssem, recv_sem=rsem,
            device_id=(grp, r, s), device_id_type=MESH,
        )

    pending = []

    loads = [
        pltpu.make_async_copy(bcw, bc_v, w_sem.at[0]),
        pltpu.make_async_copy(zxt, zx_v, w_sem.at[1]),
        pltpu.make_async_copy(ssm, ssm_v, w_sem.at[2]),
        pltpu.make_async_copy(upw, up_v, w_sem.at[3]),
        pltpu.make_async_copy(dnw, dn_v, w_sem.at[4]),
    ]

    barrier = pltpu.get_barrier_semaphore()
    for k in range(1, N):
        peer = lax.rem(me + k, N)
        pl.semaphore_signal(
            barrier, inc=1, device_id=(grp, peer // 2, peer % 2), device_id_type=MESH
        )
    for copy in loads:
        copy.start()
    hid_all[me] = hid[...]
    pl.semaphore_wait(barrier, N - 1)

    Z = R // 2
    z, x = row // 2, row % 2

    def gather_start(src, buf, ssem, rsem):
        for k in range(1, Z):
            remote(
                src, buf.at[me], ssem.at[k], rsem.at[me], lax.rem(z + k, Z) * 2 + x, sec
            ).start()
        remote(src, buf.at[me], ssem.at[0], rsem.at[me], z * 2 + 1 - x, sec).start()
        remote(src, buf.at[me], ssem.at[Z], rsem.at[me], row, other).start()

    def gather_step(j, buf, ssem, rsem):
        k, far, cross = j % Z, (j // Z) % 2, j // (2 * Z)
        blk = (lax.rem(z + k, Z) * 2 + lax.rem(x + far, 2)) * 2 + lax.rem(sec + cross, 2)
        block = buf.at[blk]

        @pl.when(j > 0)
        def _():
            remote(block, block, ssem.at[0], rsem.at[blk], row, other).wait_recv()

        @pl.when(jnp.logical_and(j > 0, j < Z))
        def _():
            remote(
                block, block, ssem.at[Z + j], rsem.at[blk], z * 2 + 1 - x, sec
            ).start()

        @pl.when(jnp.logical_and(j > 0, j < 2 * Z))
        def _():
            remote(block, block, ssem.at[2 * Z + j - 1], rsem.at[blk], row, other).start()

        return blk

    def gather_drain(buf, ssem, rsem):
        def step(i, _):
            remote(buf.at[me], buf.at[me], ssem.at[i], rsem.at[me], row, other).wait_send()
            return 0

        lax.fori_loop(0, 4 * Z - 1, step, 0)

    gather_start(hid, hid_all, h_send, h_recv)

    eye = (
        lax.broadcasted_iota(jnp.int32, (local_p, local_p), 0)
        == lax.broadcasted_iota(jnp.int32, (local_p, local_p), 1)
    ).astype(jnp.float32)

    def turn(values):
        return lax.dot_general(eye, values, NT, precision=HI, preferred_element_type=jnp.float32)

    f32 = jnp.float32
    valid_row = (valid[...] != 0).astype(f32)
    valid_col = turn(valid_row)
    pre_x = cxb[...] + sum(cxs[t].astype(f32) * cxw[t : t + 1, :] for t in range(3))
    pre_x_t = turn(pre_x)
    tap_t = turn(cxw[3:4, :])
    gnw_t = turn(gnw[...])
    pre_bc = cbb[...] + sum(cbs[t].astype(f32) * cbw[t : t + 1, :] for t in range(3))

    def add_squares(total, values):
        squares = values * values
        return total + sum(squares[:, i : i + 128] for i in range(0, wd, 128))

    def inverse(total):
        return lax.rsqrt(jnp.sum(total, axis=1, keepdims=True) / model + 1e-05)

    loads[0].wait()
    loads[1].wait()

    def project(j, carry):
        total, acc_bc, acc_zx, acc_dt = carry
        b = gather_step(j, hid_all, h_send, h_recv)
        at = pl.ds(pl.multiple_of(b * wd, wd), wd)
        values = hid_all[b].astype(f32)
        total = add_squares(total, values)
        fed = (values * gin[:, at]).astype(jnp.bfloat16)
        acc_bc += jnp.dot(fed, bc_v[at, :], preferred_element_type=f32)
        acc_zx += lax.dot_general(zx_v[:, at], fed, NT, preferred_element_type=f32)
        dt_rows = jnp.broadcast_to(dtt[:, at].astype(f32), (16, wd)).astype(jnp.bfloat16)
        acc_dt += lax.dot_general(dt_rows, fed, NT, preferred_element_type=f32)
        return total, acc_bc, acc_zx, acc_dt

    total, acc_bc, acc_zx, acc_dt = lax.fori_loop(
        0, N, project,
        (
            jnp.zeros((rows, 128), f32),
            jnp.zeros((rows, bc_v.shape[1]), f32),
            jnp.zeros((2 * local_p, rows), f32),
            jnp.zeros((16, rows), f32),
        ),
    )
    scale = inverse(total)
    eye_rows = (
        lax.broadcasted_iota(jnp.int32, (rows, rows), 0)
        == lax.broadcasted_iota(jnp.int32, (rows, rows), 1)
    ).astype(f32)
    scale_row = jnp.sum(eye_rows * scale, axis=0, keepdims=True)
    acc_bc, acc_zx, acc_dt = acc_bc * scale, acc_zx * scale_row, acc_dt * scale_row
    bc_pre = acc_bc.astype(jnp.bfloat16).astype(f32)
    mixed_bc = silu(pre_bc + bc_pre * cbw[3:4, :])
    bc_out[...] = mixed_bc

    cb = bc_v.shape[1]
    parts = STATE // cb
    half = me // (N // 2)
    to_group = lax.rem(me, N // 2) // parts
    slot = half * parts + lax.rem(me, parts)
    per = N // GROUPS
    my_group = me // per
    for i in range(per):
        dest = to_group * per + i

        @pl.when(dest != me)
        def _():
            remote(
                bc_out, bc_all.at[slot], bc_send.at[i], bc_recv.at[slot], dest // 2, dest % 2
            ).start()

        @pl.when(dest == me)
        def _():
            bc_all[slot] = bc_out[...]

    place = x * 2 + sec
    spots = [(1 - x, sec), (row % 2, other), (1 - x, other)]
    for i, (px, pc) in enumerate(spots):
        for t in range(Z):
            at = pl.ds(pl.multiple_of((t * 4 + px * 2 + pc) * wd, wd), wd)
            copy = remote(
                outw.at[:, at], owt.at[t * 4 + place], o_send.at[i * Z + t],
                o_recv.at[t * 4 + place], z * 2 + px, pc,
            )
            copy.start()
            pending.append(copy)
    own_w = []
    for t in range(Z):
        at = pl.ds(pl.multiple_of((t * 4 + place) * wd, wd), wd)
        own_w.append(
            pltpu.make_async_copy(outw.at[:, at], owt.at[t * 4 + place], w_sem.at[6 + t])
        )
        own_w[-1].start()

    gate_t = silu(acc_zx[:local_p])
    inner_pre_t = acc_zx[local_p:].astype(jnp.bfloat16).astype(f32)
    inner_t = silu(pre_x_t + inner_pre_t * tap_t)
    dt_sum = acc_dt[0:1] + dtb[...]
    step_size = jnp.maximum(dt_sum, 0.0) + jnp.log1p(jnp.exp(-jnp.abs(dt_sum)))
    decay = jnp.exp(-step_size * jnp.exp(dlog[...]))
    driven_t = inner_t * step_size
    keep_x = jnp.broadcast_to(valid_col, (rows, local_p)) > 0.5
    keep_bc = jnp.broadcast_to(valid_col, (rows, cb)) > 0.5
    last_x = turn(inner_pre_t)
    for t in range(3):
        later_x = last_x if t == 2 else cxs[t + 1].astype(f32)
        later_bc = bc_pre if t == 2 else cbs[t + 1].astype(f32)
        new_cx[t] = jnp.where(keep_x, later_x, cxs[t].astype(f32)).astype(jnp.bfloat16)
        new_cb[t] = jnp.where(keep_bc, later_bc, cbs[t].astype(f32)).astype(jnp.bfloat16)
    loads[2].wait()

    for h in range(2):
        for p in range(parts):
            source = h * (N // 2) + my_group * parts + p

            @pl.when(source != me)
            def _():
                remote(
                    bc_out, bc_all.at[h * parts + p], bc_send.at[0], bc_recv.at[h * parts + p],
                    row, other,
                ).wait_recv()

    state_in = jnp.concatenate([bc_all[p] for p in range(parts)], axis=1)
    state_out = jnp.concatenate([bc_all[parts + p] for p in range(parts)], axis=1)

    lane = lax.broadcasted_iota(jnp.int32, (local_p, rows), 1)

    def updated(r):
        previous = ssm_v[r].astype(f32)
        value = decay[0:1, r : r + 1] * previous + driven_t[:, r : r + 1] * state_in[r : r + 1, :]
        return previous, value

    read_t = jnp.zeros((local_p, rows), f32)
    for r in range(rows):
        _, value = updated(r)
        column = jnp.sum(value * state_out[r : r + 1, :], axis=1, keepdims=True)
        read_t = jnp.where(lane == r, column, read_t)
    gated_t = (read_t + skip[...] * inner_t) * gate_t
    g_out[:, 0:rows] = gated_t
    g_out[:, rows : rows + 1] = gnw_t
    for i, (px, pc) in enumerate(spots):
        copy = remote(
            g_out, g_all.at[place], g_send.at[i], g_recv.at[place], z * 2 + px, pc
        )
        copy.start()
        pending.append(copy)
    g_all[place] = g_out[...]

    for r in range(rows):
        previous, value = updated(r)
        keep = jnp.broadcast_to(valid_row[0:1, r : r + 1], value.shape) > 0.5
        ssm_v[r] = jnp.where(keep, value, previous).astype(jnp.bfloat16)
    store_ssm = pltpu.make_async_copy(ssm_v, new_ssm, w_sem.at[5])
    store_ssm.start()

    for copy in own_w:
        copy.wait()
    for px, pc in spots:
        there = px * 2 + pc
        for t in range(Z):
            spot = t * 4 + there
            remote(
                owt.at[spot], owt.at[spot], o_send.at[0], o_recv.at[spot], row, other
            ).wait_recv()
    for px, pc in spots:
        there = px * 2 + pc
        remote(
            g_all.at[there], g_all.at[there], g_send.at[0], g_recv.at[there], row, other
        ).wait_recv()

    pieces = [g_all[i, :, 0:rows] for i in range(4)]
    squares = sum(jnp.sum(piece * piece, axis=0, keepdims=True) for piece in pieces)
    norm = lax.rsqrt(squares / (4 * local_p) + 1e-05)
    scaled_t = jnp.concatenate(
        [pieces[i] * norm * g_all[i, :, rows : rows + 1] for i in range(4)], axis=0
    ).astype(jnp.bfloat16)
    scaled = lax.dot_general(
        eye_rows.astype(jnp.bfloat16), scaled_t, NT, preferred_element_type=f32
    ).astype(jnp.bfloat16)

    def mixer(t):
        weights = owt[pl.ds(t * 4, 4)].reshape(4 * local_p, wd)
        return jnp.dot(scaled, weights, preferred_element_type=f32)

    for k in (2, 1, 3):
        t = lax.rem(z + k, Z)
        send_m[k] = mixer(t).astype(jnp.bfloat16)
        copy = remote(
            send_m.at[k], recv_m.at[z], x_send.at[k], x_recv.at[z], t * 2 + x, sec
        )
        copy.start()
        pending.append(copy)
    mixed = hid[...].astype(f32) + mixer(z)
    for k in (1, 3, 2):
        t = lax.rem(z + k, Z)
        remote(
            recv_m.at[t], recv_m.at[t], x_send.at[0], x_recv.at[t], row, other
        ).wait_recv()
        mixed += recv_m[t].astype(f32)
    mid[...] = mixed.astype(jnp.bfloat16)
    gather_start(mid, mid_all, m_send, m_recv)
    mid_all[me] = mid[...]
    loads[3].wait()
    act[...] = jnp.zeros_like(act)

    def up_step(j, total):
        b = gather_step(j, mid_all, m_send, m_recv)
        at = pl.ds(pl.multiple_of(b * wd, wd), wd)
        values = mid_all[b].astype(f32)
        fed = (values * gmid[:, at]).astype(jnp.bfloat16)
        act[...] += jnp.dot(fed, up_v[at, :], preferred_element_type=f32)
        return add_squares(total, values)

    total = lax.fori_loop(0, N, up_step, jnp.zeros((rows, 128), f32))
    activated = jnp.square(jnp.maximum(act[...] * inverse(total), 0.0)).astype(jnp.bfloat16)
    loads[4].wait()

    def down(block):
        at = pl.ds(pl.multiple_of(block * wd, wd), wd)
        return jnp.dot(activated, dn_v[:, at], preferred_element_type=f32)

    def for_partner(k, _):
        target = lax.rem(row + 1 + k, R)
        send_a[k] = down(target * 2 + other).astype(jnp.bfloat16)
        remote(send_a.at[k], recv_a.at[k], a_send.at[k], a_recv.at[k], row, other).start()
        return 0

    lax.fori_loop(0, R, for_partner, 0)

    def for_chip(k, _):
        target = lax.rem(row + 1 + k, R)
        part = down(target * 2 + sec)
        remote(send_a.at[k], recv_a.at[k], a_send.at[k], a_recv.at[k], row, other).wait()
        send_b[k] = (part + recv_a[k].astype(f32)).astype(jnp.bfloat16)
        remote(send_b.at[k], recv_b.at[row], b_send.at[k], b_recv.at[row], target, sec).start()
        return 0

    lax.fori_loop(0, R - 1, for_chip, 0)
    total = down(me)
    remote(
        send_a.at[R - 1], recv_a.at[R - 1], a_send.at[R - 1], a_recv.at[R - 1], row, other
    ).wait()
    own_sum[...] = total + recv_a[R - 1].astype(f32) + mid[...].astype(f32)

    def collect(k, _):
        source = lax.rem(row + R - 1 - k, R)
        remote(
            send_b.at[k], recv_b.at[source], b_send.at[k], b_recv.at[source], source, sec
        ).wait_recv()
        own_sum[...] += recv_b[source].astype(f32)
        return 0

    lax.fori_loop(0, R - 1, collect, 0)
    out[...] = own_sum[...].astype(jnp.bfloat16)

    def drain(k, _):
        remote(
            send_b.at[k], recv_b.at[row], b_send.at[k], b_recv.at[row], row, other
        ).wait_send()
        return 0

    lax.fori_loop(0, R - 1, drain, 0)
    for i in range(per):
        dest = to_group * per + i

        @pl.when(dest != me)
        def _():
            remote(
                bc_out, bc_all.at[slot], bc_send.at[i], bc_recv.at[slot], row, other
            ).wait_send()

    for copy in pending:
        copy.wait_send()
    gather_drain(hid_all, h_send, h_recv)
    gather_drain(mid_all, m_send, m_recv)
    store_ssm.wait()


def hand_over(*refs):
    count = (len(refs) - 2) // 3
    ins, outs, held = refs[:count], refs[count : 2 * count], refs[2 * count : 3 * count]
    in_sem, out_sem = refs[3 * count], refs[3 * count + 1]
    parts = []
    for i in range(count):
        cuts = 4 if i == 1 else 1
        size = ins[i].shape[0] // cuts
        for c in range(cuts):
            at = pl.ds(c * size, size)
            n = len(parts)
            parts.append(
                (
                    pltpu.make_async_copy(ins[i].at[at], held[i].at[at], in_sem.at[n]),
                    pltpu.make_async_copy(held[i].at[at], outs[i].at[at], out_sem.at[n]),
                )
            )
    for first, _ in parts:
        first.start()
    for first, second in parts:
        first.wait()
        second.start()
    for _, second in parts:
        second.wait()


def fused_body(
    hidden, norm_in_gain, zx_weight, bc_weight, dt_weight, dt_bias, decay_log, skip_gain,
    conv_x_weight, conv_x_bias, conv_bc_weight, conv_bc_bias, conv_x_state, conv_bc_state,
    ssm_state, gate_norm_weight, out_weight, norm_mid_gain, up_weight, down_weight, valid,
):
    R = lax.axis_size("row")
    N = 2 * R
    rows, wd = hidden.shape
    model = up_weight.shape[0]
    p = zx_weight.shape[3]
    cb = bc_weight.shape[1]
    ff = up_weight.shape[1]
    bf16, f32 = jnp.bfloat16, jnp.float32
    vm, hbm = pl.BlockSpec(memory_space=pltpu.VMEM), pl.BlockSpec(memory_space=pl.ANY)
    dma = pltpu.SemaphoreType.DMA
    results = pl.pallas_call(
        functools.partial(fused_kernel, R),
        out_shape=(
            jax.ShapeDtypeStruct((rows, wd), bf16),
            jax.ShapeDtypeStruct((rows, p, STATE), bf16),
            jax.ShapeDtypeStruct((3, rows, p), bf16),
            jax.ShapeDtypeStruct((3, rows, cb), bf16),
        ),
        in_specs=[
            vm, vm, hbm, hbm, vm, vm, vm, vm, vm, vm, vm, vm, vm, vm, hbm, vm, hbm, vm, hbm, hbm, vm
        ],
        out_specs=(vm, hbm, vm, vm),
        scratch_shapes=[
            pltpu.VMEM((2 * p, model), bf16),
            pltpu.VMEM((model, cb), bf16),
            pltpu.VMEM((rows, p, STATE), bf16),
            pltpu.VMEM((model, ff), bf16),
            pltpu.VMEM((ff, model), bf16),
            pltpu.VMEM((N, rows, wd), bf16),
            pltpu.VMEM((N, p, wd), bf16),
            pltpu.VMEM((rows, cb), f32),
            pltpu.VMEM((2 * STATE // cb, rows, cb), f32),
            pltpu.VMEM((p, 128), f32),
            pltpu.VMEM((4, p, 128), f32),
            pltpu.VMEM((rows, wd), bf16),
            pltpu.VMEM((N, rows, wd), bf16),
            pltpu.VMEM((R // 2, rows, wd), bf16),
            pltpu.VMEM((R // 2, rows, wd), bf16),
            pltpu.VMEM((rows, ff), f32),
            pltpu.VMEM((R, rows, wd), bf16),
            pltpu.VMEM((R, rows, wd), bf16),
            pltpu.VMEM((R, rows, wd), bf16),
            pltpu.VMEM((R, rows, wd), bf16),
            pltpu.VMEM((rows, wd), f32),
            dma((6 + R // 2,)), dma((N,)), dma((N,)), dma((N,)), dma((N,)),
            dma((N // GROUPS,)), dma((2 * STATE // cb,)),
            dma((N,)), dma((N,)), dma((N,)), dma((N,)),
            dma((R,)), dma((R,)), dma((R,)), dma((R,)), dma((R,)), dma((R,)),
        ],
        compiler_params=pltpu.CompilerParams(
            collective_id=0, has_side_effects=True, vmem_limit_bytes=60 * 1024 * 1024
        ),
    )(
        hidden,
        norm_in_gain.reshape(1, model),
        jnp.transpose(zx_weight, (1, 2, 3, 0)).reshape(2 * p, model),
        bc_weight,
        dt_weight.reshape(1, model),
        dt_bias.reshape(1, 1),
        decay_log.reshape(1, 1),
        skip_gain.reshape(1, 1),
        conv_x_weight.reshape(4, p),
        conv_x_bias.reshape(1, p),
        conv_bc_weight,
        conv_bc_bias.reshape(1, cb),
        jnp.transpose(conv_x_state, (1, 2, 0, 3)).reshape(3, rows, p),
        jnp.transpose(conv_bc_state, (1, 0, 2)),
        ssm_state.reshape(rows, p, STATE),
        gate_norm_weight.reshape(1, p),
        out_weight.reshape(p, model),
        norm_mid_gain.reshape(1, model),
        up_weight,
        down_weight,
        valid.reshape(1, rows),
    )
    out, new_ssm, new_cx, new_cb = pl.pallas_call(
        hand_over,
        out_shape=tuple(jax.ShapeDtypeStruct(v.shape, v.dtype) for v in results),
        in_specs=[hbm] * 4,
        out_specs=(hbm,) * 4,
        scratch_shapes=[pltpu.VMEM(v.shape, v.dtype) for v in results] + [dma((7,)), dma((7,))],
    )(*results)
    return (
        out,
        new_ssm.reshape(rows, 1, p, STATE),
        jnp.transpose(new_cx, (1, 0, 2)).reshape(rows, 3, 1, p),
        jnp.transpose(new_cb, (1, 0, 2)),
    )


def solution(mesh):
    chosen = fused_body if fits(mesh) else body
    return jax.shard_map(
        chosen,
        mesh=mesh,
        in_specs=(
            P("groups", ("row", "section")),
            P(),
            P(None, None, "row", "section"),
            P(None, ("row", "section")),
            P(None, "row"),
            P("row"),
            P("row"),
            P("row"),
            P(None, "row", "section"),
            P("row", "section"),
            P(None, ("row", "section")),
            P(("row", "section")),
            P("groups", None, "row", "section"),
            P("groups", None, ("row", "section")),
            P("groups", "row", "section", None),
            P("row", "section"),
            P("row", "section", None),
            P(),
            P(None, ("row", "section")),
            P(("row", "section"), None),
            P("groups"),
        ),
        out_specs=(
            P("groups", ("row", "section")),
            P("groups", "row", "section", None),
            P("groups", None, "row", "section"),
            P("groups", None, ("row", "section")),
        ),
        check_vma=False,
    )
```

```python
import functools

import jax
import jax.numpy as jnp
from jax import lax
from jax.experimental import pallas as pl
from jax.experimental.pallas import tpu as pltpu
from jax.sharding import PartitionSpec as P

D = 8192
HEAD_DIM = 64
STATE = 256
GROUPS = 4


def mean_norm(values, gain):
    return values * lax.rsqrt(jnp.mean(values * values, axis=-1, keepdims=True) + 1e-05) * gain


def body(
    hidden,
    norm_in_gain,
    zx_weight,
    bc_weight,
    dt_weight,
    dt_bias,
    decay_log,
    skip_gain,
    conv_x_weight,
    conv_x_bias,
    conv_bc_weight,
    conv_bc_bias,
    conv_x_state,
    conv_bc_state,
    ssm_state,
    gate_norm_weight,
    out_weight,
    norm_mid_gain,
    up_weight,
    down_weight,
    valid,
):
    row_count = hidden.shape[0]
    local_p = zx_weight.shape[3]
    full_rows = lax.all_gather(hidden, ("row", "section"), axis=1, tiled=True)
    normed = mean_norm(full_rows.astype(jnp.float32), norm_in_gain).astype(jnp.bfloat16)
    gate_inner = jnp.dot(
        normed, zx_weight.reshape(D, 2 * local_p), preferred_element_type=jnp.float32
    ).reshape(row_count, 2, 1, local_p)
    gate_part = gate_inner[:, 0]
    inner_pre = gate_inner[:, 1].astype(jnp.bfloat16)
    bc_pre = jnp.dot(normed, bc_weight, preferred_element_type=jnp.float32).astype(jnp.bfloat16)
    dt_raw = jnp.dot(normed, dt_weight, preferred_element_type=jnp.float32)
    taps_x = jnp.concatenate([conv_x_state, inner_pre[:, None]], axis=1)
    inner = jax.nn.silu(
        jnp.sum(taps_x.astype(jnp.float32) * conv_x_weight[None], axis=1) + conv_x_bias
    )
    taps_bc = jnp.concatenate([conv_bc_state, bc_pre[:, None]], axis=1)
    mixed_bc = jax.nn.silu(
        jnp.sum(taps_bc.astype(jnp.float32) * conv_bc_weight[None], axis=1) + conv_bc_bias
    )
    all_bc = lax.all_gather(mixed_bc, ("row", "section"), axis=1, tiled=True)
    per_group = lax.axis_size("row") // GROUPS
    group_index = lax.axis_index("row") // per_group
    state_in = all_bc[:, : GROUPS * STATE].reshape(row_count, GROUPS, STATE)
    state_out = all_bc[:, GROUPS * STATE :].reshape(row_count, GROUPS, STATE)
    in_mine = lax.dynamic_slice_in_dim(state_in, group_index, 1, axis=1)
    out_mine = lax.dynamic_slice_in_dim(state_out, group_index, 1, axis=1)
    step_size = jax.nn.softplus(dt_raw + dt_bias[None])
    decay_rate = jnp.exp(-step_size * jnp.exp(decay_log)[None])
    previous = ssm_state.astype(jnp.float32)
    updated = (
        decay_rate[:, :, None, None] * previous
        + (step_size[:, :, None] * inner)[..., None] * in_mine[:, :, None, :]
    )
    readout = (
        jnp.einsum("rhpn,rhn->rhp", updated, out_mine, precision=lax.Precision.HIGHEST)
        + skip_gain[None, :, None] * inner
    )
    gated = readout * jax.nn.silu(gate_part)
    local_squares = jnp.sum(gated * gated, axis=(1, 2))
    group_pick = (jnp.arange(GROUPS) == group_index).astype(jnp.float32)
    group_sums = lax.psum(local_squares[:, None] * group_pick[None], ("row", "section"))
    group_size = per_group * HEAD_DIM
    group_mean = jnp.sum(group_sums * group_pick[None], axis=1) / group_size
    scaled = (gated * lax.rsqrt(group_mean + 1e-05)[:, None, None] * gate_norm_weight[None]).astype(
        jnp.bfloat16
    )
    mixer_terms = jnp.dot(
        scaled.reshape(row_count, local_p),
        out_weight.reshape(local_p, D),
        preferred_element_type=jnp.float32,
    )
    mixer_share = lax.psum_scatter(mixer_terms, ("row", "section"), scatter_dimension=1, tiled=True)
    middle = (hidden.astype(jnp.float32) + mixer_share).astype(jnp.bfloat16)
    middle_full = lax.all_gather(middle, ("row", "section"), axis=1, tiled=True)
    mlp_in = mean_norm(middle_full.astype(jnp.float32), norm_mid_gain).astype(jnp.bfloat16)
    up_values = jnp.dot(mlp_in, up_weight, preferred_element_type=jnp.float32)
    activated = jnp.square(jax.nn.relu(up_values)).astype(jnp.bfloat16)
    down_terms = jnp.dot(activated, down_weight, preferred_element_type=jnp.float32)
    down_share = lax.psum_scatter(down_terms, ("row", "section"), scatter_dimension=1, tiled=True)
    block_out = (middle.astype(jnp.float32) + down_share).astype(jnp.bfloat16)
    kept_rows = valid != 0
    new_ssm_state = jnp.where(kept_rows[:, None, None, None], updated, previous).astype(
        jnp.bfloat16
    )
    new_conv_x_state = jnp.where(kept_rows[:, None, None, None], taps_x[:, 1:], conv_x_state)
    new_conv_bc_state = jnp.where(kept_rows[:, None, None], taps_bc[:, 1:], conv_bc_state)
    return (block_out, new_ssm_state, new_conv_x_state, new_conv_bc_state)


HI = lax.Precision.HIGHEST
MESH = pl.DeviceIdType.MESH
NT = (((1,), (1,)), ((), ()))


def fits(mesh):
    return mesh.shape["section"] == 2 and mesh.shape["row"] == 2 * GROUPS


def silu(values):
    return values / (1.0 + jnp.exp(-values))


SMALL = (0, 1, 4, 5, 6, 7, 8, 9, 10, 11, 12, 13, 15, 17, 20)


def staged_kernel(R, *refs):
    count = len(SMALL)
    ins, rest, held, sem = list(refs[:21]), refs[21 : -count - 1], refs[-count - 1 : -1], refs[-1]
    copies = [pltpu.make_async_copy(ins[i], held[n], sem.at[n]) for n, i in enumerate(SMALL)]
    hid_source = ins[0]
    for n, i in enumerate(SMALL):
        ins[i] = held[n]
    fused_kernel(R, copies, hid_source, *ins, *rest)


def fused_kernel(
    R, small_copies, hid_source,
    hid, gin, zxt, bcw, dtt, dtb, dlog, skip, cxw, cxb, cbw, cbb, cxs, cbs, ssm, gnw, outw, gmid,
    upw, dnw, valid,
    out, new_ssm, new_cx, new_cb,
    zx_v, bc_v, ssm_v, up_v, dn_v, hid_all, owt, bc_out, bc_all, g_out, g_all, mid, mid_all,
    send_m, recv_m, act, send_a, recv_a, send_b, recv_b, own_sum,
    w_sem, h_send, h_recv, o_send, o_recv, bc_send, bc_recv, g_send, g_recv, m_send, m_recv,
    a_send, a_recv, b_send, b_recv, x_send, x_recv,
):
    N = 2 * R
    grp, row, sec = lax.axis_index("groups"), lax.axis_index("row"), lax.axis_index("section")
    me = row * 2 + sec
    other = 1 - sec
    rows, wd = hid.shape
    local_p = zxt.shape[0] // 2
    model = upw.shape[0]

    def remote(src, dst, ssem, rsem, r, s):
        return pltpu.make_async_remote_copy(
            src_ref=src, dst_ref=dst, send_sem=ssem, recv_sem=rsem,
            device_id=(grp, r, s), device_id_type=MESH,
        )

    pending = []

    loads = [
        pltpu.make_async_copy(bcw, bc_v, w_sem.at[0]),
        pltpu.make_async_copy(zxt, zx_v, w_sem.at[1]),
        pltpu.make_async_copy(ssm, ssm_v, w_sem.at[2]),
        pltpu.make_async_copy(upw, up_v, w_sem.at[3]),
        pltpu.make_async_copy(dnw, dn_v, w_sem.at[4]),
    ]

    barrier = pltpu.get_barrier_semaphore()
    for k in range(1, N):
        peer = lax.rem(me + k, N)
        pl.semaphore_signal(
            barrier, inc=1, device_id=(grp, peer // 2, peer % 2), device_id_type=MESH
        )
    for copy in small_copies + loads:
        copy.start()
    pl.semaphore_wait(barrier, N - 1)

    Z = R // 2
    z, x = row // 2, row % 2

    def gather_start(src, buf, ssem, rsem):
        for k in range(1, Z):
            remote(
                src, buf.at[me], ssem.at[k], rsem.at[me], lax.rem(z + k, Z) * 2 + x, sec
            ).start()
        remote(src, buf.at[me], ssem.at[0], rsem.at[me], z * 2 + 1 - x, sec).start()
        remote(src, buf.at[me], ssem.at[Z], rsem.at[me], row, other).start()

    visits = (0, 8, 4, 1, 3, 12, 5, 7, 2, 9, 11, 6, 13, 15, 10, 14)

    def gather_step(i, buf, ssem, rsem):
        j = jnp.int32(0)
        for position, visit in enumerate(visits):
            j = jnp.where(i == position, visit, j)
        k, far, cross = j % Z, (j // Z) % 2, j // (2 * Z)
        blk = (lax.rem(z + k, Z) * 2 + lax.rem(x + far, 2)) * 2 + lax.rem(sec + cross, 2)
        block = buf.at[blk]

        @pl.when(j > 0)
        def _():
            remote(block, block, ssem.at[0], rsem.at[blk], row, other).wait_recv()

        @pl.when(jnp.logical_and(j > 0, j < Z))
        def _():
            remote(
                block, block, ssem.at[Z + j], rsem.at[blk], z * 2 + 1 - x, sec
            ).start()

        @pl.when(jnp.logical_and(j > 0, j < 2 * Z))
        def _():
            remote(block, block, ssem.at[2 * Z + j - 1], rsem.at[blk], row, other).start()

        return blk

    def gather_drain(buf, ssem, rsem):
        def step(i, _):
            remote(buf.at[me], buf.at[me], ssem.at[i], rsem.at[me], row, other).wait_send()
            return 0

        lax.fori_loop(0, 4 * Z - 1, step, 0)

    gather_start(hid_source, hid_all, h_send, h_recv)
    for copy in small_copies:
        copy.wait()
    hid_all[me] = hid[...]

    eye = (
        lax.broadcasted_iota(jnp.int32, (local_p, local_p), 0)
        == lax.broadcasted_iota(jnp.int32, (local_p, local_p), 1)
    ).astype(jnp.float32)

    def turn(values):
        return lax.dot_general(eye, values, NT, precision=HI, preferred_element_type=jnp.float32)

    f32 = jnp.float32
    valid_row = (valid[...] != 0).astype(f32)
    valid_col = turn(valid_row)
    pre_x = cxb[...] + sum(cxs[t].astype(f32) * cxw[t : t + 1, :] for t in range(3))
    pre_x_t = turn(pre_x)
    tap_t = turn(cxw[3:4, :])
    gnw_t = turn(gnw[...])
    pre_bc = cbb[...] + sum(cbs[t].astype(f32) * cbw[t : t + 1, :] for t in range(3))

    def add_squares(total, values):
        squares = values * values
        return total + sum(squares[:, i : i + 128] for i in range(0, wd, 128))

    def inverse(total):
        return lax.rsqrt(jnp.sum(total, axis=1, keepdims=True) / model + 1e-05)

    loads[0].wait()
    loads[1].wait()

    def project(j, carry):
        total, acc_bc, acc_zx, acc_dt = carry
        b = gather_step(j, hid_all, h_send, h_recv)
        at = pl.ds(pl.multiple_of(b * wd, wd), wd)
        values = hid_all[b].astype(f32)
        total = add_squares(total, values)
        fed = (values * gin[:, at]).astype(jnp.bfloat16)
        acc_bc += jnp.dot(fed, bc_v[at, :], preferred_element_type=f32)
        acc_zx += lax.dot_general(zx_v[:, at], fed, NT, preferred_element_type=f32)
        dt_rows = jnp.broadcast_to(dtt[:, at].astype(f32), (16, wd)).astype(jnp.bfloat16)
        acc_dt += lax.dot_general(dt_rows, fed, NT, preferred_element_type=f32)
        return total, acc_bc, acc_zx, acc_dt

    total, acc_bc, acc_zx, acc_dt = lax.fori_loop(
        0, N, project,
        (
            jnp.zeros((rows, 128), f32),
            jnp.zeros((rows, bc_v.shape[1]), f32),
            jnp.zeros((2 * local_p, rows), f32),
            jnp.zeros((16, rows), f32),
        ),
    )
    scale = inverse(total)
    eye_rows = (
        lax.broadcasted_iota(jnp.int32, (rows, rows), 0)
        == lax.broadcasted_iota(jnp.int32, (rows, rows), 1)
    ).astype(f32)
    scale_row = jnp.sum(eye_rows * scale, axis=0, keepdims=True)
    acc_bc, acc_zx, acc_dt = acc_bc * scale, acc_zx * scale_row, acc_dt * scale_row
    bc_pre = acc_bc.astype(jnp.bfloat16).astype(f32)
    mixed_bc = silu(pre_bc + bc_pre * cbw[3:4, :])
    bc_out[...] = mixed_bc

    cb = bc_v.shape[1]
    parts = STATE // cb
    half = me // (N // 2)
    to_group = lax.rem(me, N // 2) // parts
    slot = half * parts + lax.rem(me, parts)
    per = N // GROUPS
    my_group = me // per
    for i in range(per):
        dest = to_group * per + i

        @pl.when(dest != me)
        def _():
            remote(
                bc_out, bc_all.at[slot], bc_send.at[i], bc_recv.at[slot], dest // 2, dest % 2
            ).start()

        @pl.when(dest == me)
        def _():
            bc_all[slot] = bc_out[...]

    place = x * 2 + sec
    spots = [(1 - x, sec), (row % 2, other), (1 - x, other)]
    for i, (px, pc) in enumerate(spots):
        for t in range(Z):
            at = pl.ds(pl.multiple_of((t * 4 + px * 2 + pc) * wd, wd), wd)
            copy = remote(
                outw.at[:, at], owt.at[t * 4 + place], o_send.at[i * Z + t],
                o_recv.at[t * 4 + place], z * 2 + px, pc,
            )
            copy.start()
            pending.append(copy)
    own_w = []
    for t in range(Z):
        at = pl.ds(pl.multiple_of((t * 4 + place) * wd, wd), wd)
        own_w.append(
            pltpu.make_async_copy(outw.at[:, at], owt.at[t * 4 + place], w_sem.at[6 + t])
        )
        own_w[-1].start()

    gate_t = silu(acc_zx[:local_p])
    inner_pre_t = acc_zx[local_p:].astype(jnp.bfloat16).astype(f32)
    inner_t = silu(pre_x_t + inner_pre_t * tap_t)
    dt_sum = acc_dt[0:1] + dtb[...]
    step_size = jnp.maximum(dt_sum, 0.0) + jnp.log1p(jnp.exp(-jnp.abs(dt_sum)))
    decay = jnp.exp(-step_size * jnp.exp(dlog[...]))
    driven_t = inner_t * step_size
    keep_x = jnp.broadcast_to(valid_col, (rows, local_p)) > 0.5
    keep_bc = jnp.broadcast_to(valid_col, (rows, cb)) > 0.5
    last_x = turn(inner_pre_t)
    for t in range(3):
        later_x = last_x if t == 2 else cxs[t + 1].astype(f32)
        later_bc = bc_pre if t == 2 else cbs[t + 1].astype(f32)
        new_cx[t] = jnp.where(keep_x, later_x, cxs[t].astype(f32)).astype(jnp.bfloat16)
        new_cb[t] = jnp.where(keep_bc, later_bc, cbs[t].astype(f32)).astype(jnp.bfloat16)
    loads[2].wait()

    for h in range(2):
        for p in range(parts):
            source = h * (N // 2) + my_group * parts + p

            @pl.when(source != me)
            def _():
                remote(
                    bc_out, bc_all.at[h * parts + p], bc_send.at[0], bc_recv.at[h * parts + p],
                    row, other,
                ).wait_recv()

    state_in = jnp.concatenate([bc_all[p] for p in range(parts)], axis=1)
    state_out = jnp.concatenate([bc_all[parts + p] for p in range(parts)], axis=1)

    lane = lax.broadcasted_iota(jnp.int32, (local_p, rows), 1)

    def updated(r):
        previous = ssm_v[r].astype(f32)
        value = decay[0:1, r : r + 1] * previous + driven_t[:, r : r + 1] * state_in[r : r + 1, :]
        return previous, value

    read_t = jnp.zeros((local_p, rows), f32)
    for r in range(rows):
        _, value = updated(r)
        column = jnp.sum(value * state_out[r : r + 1, :], axis=1, keepdims=True)
        read_t = jnp.where(lane == r, column, read_t)
    gated_t = (read_t + skip[...] * inner_t) * gate_t
    g_out[:, 0:rows] = gated_t
    g_out[:, rows : rows + 1] = gnw_t
    for i, (px, pc) in enumerate(spots):
        copy = remote(
            g_out, g_all.at[place], g_send.at[i], g_recv.at[place], z * 2 + px, pc
        )
        copy.start()
        pending.append(copy)
    g_all[place] = g_out[...]

    for r in range(rows):
        previous, value = updated(r)
        keep = jnp.broadcast_to(valid_row[0:1, r : r + 1], value.shape) > 0.5
        ssm_v[r] = jnp.where(keep, value, previous).astype(jnp.bfloat16)
    store_ssm = pltpu.make_async_copy(ssm_v, new_ssm, w_sem.at[5])
    store_ssm.start()

    for copy in own_w:
        copy.wait()
    for px, pc in spots:
        there = px * 2 + pc
        for t in range(Z):
            spot = t * 4 + there
            remote(
                owt.at[spot], owt.at[spot], o_send.at[0], o_recv.at[spot], row, other
            ).wait_recv()
    for px, pc in spots:
        there = px * 2 + pc
        remote(
            g_all.at[there], g_all.at[there], g_send.at[0], g_recv.at[there], row, other
        ).wait_recv()

    pieces = [g_all[i, :, 0:rows] for i in range(4)]
    squares = sum(jnp.sum(piece * piece, axis=0, keepdims=True) for piece in pieces)
    norm = lax.rsqrt(squares / (4 * local_p) + 1e-05)
    scaled_t = jnp.concatenate(
        [pieces[i] * norm * g_all[i, :, rows : rows + 1] for i in range(4)], axis=0
    ).astype(jnp.bfloat16)
    scaled = lax.dot_general(
        eye_rows.astype(jnp.bfloat16), scaled_t, NT, preferred_element_type=f32
    ).astype(jnp.bfloat16)

    def mixer(t):
        weights = owt[pl.ds(t * 4, 4)].reshape(4 * local_p, wd)
        return jnp.dot(scaled, weights, preferred_element_type=f32)

    for k in (2, 1, 3):
        t = lax.rem(z + k, Z)
        send_m[k] = mixer(t).astype(jnp.bfloat16)
        copy = remote(
            send_m.at[k], recv_m.at[z], x_send.at[k], x_recv.at[z], t * 2 + x, sec
        )
        copy.start()
        pending.append(copy)
    mixed = hid[...].astype(f32) + mixer(z)
    for k in (1, 3, 2):
        t = lax.rem(z + k, Z)
        remote(
            recv_m.at[t], recv_m.at[t], x_send.at[0], x_recv.at[t], row, other
        ).wait_recv()
        mixed += recv_m[t].astype(f32)
    mid[...] = mixed.astype(jnp.bfloat16)
    gather_start(mid, mid_all, m_send, m_recv)
    mid_all[me] = mid[...]
    loads[3].wait()
    act[...] = jnp.zeros_like(act)

    def up_step(j, total):
        b = gather_step(j, mid_all, m_send, m_recv)
        at = pl.ds(pl.multiple_of(b * wd, wd), wd)
        values = mid_all[b].astype(f32)
        fed = (values * gmid[:, at]).astype(jnp.bfloat16)
        act[...] += jnp.dot(fed, up_v[at, :], preferred_element_type=f32)
        return add_squares(total, values)

    total = lax.fori_loop(0, N, up_step, jnp.zeros((rows, 128), f32))
    activated = jnp.square(jnp.maximum(act[...] * inverse(total), 0.0)).astype(jnp.bfloat16)
    loads[4].wait()

    def down(block):
        at = pl.ds(pl.multiple_of(block * wd, wd), wd)
        return jnp.dot(activated, dn_v[:, at], preferred_element_type=f32)

    def target_of(k):
        hop = jnp.where(k < 2, 2, jnp.where(k < 4, 1, jnp.where(k < 6, 3, 0)))
        return lax.rem(z + hop, Z) * 2 + lax.rem(x + 1 + k, 2)

    def for_partner(k):
        send_a[k] = down(target_of(k) * 2 + other).astype(jnp.bfloat16)
        remote(send_a.at[k], recv_a.at[k], a_send.at[k], a_recv.at[k], row, other).start()

    def for_chip(k):
        target = target_of(k)
        part = down(target * 2 + sec)
        remote(send_a.at[k], recv_a.at[k], a_send.at[k], a_recv.at[k], row, other).wait()
        send_b[k] = (part + recv_a[k].astype(f32)).astype(jnp.bfloat16)
        remote(send_b.at[k], recv_b.at[row], b_send.at[k], b_recv.at[row], target, sec).start()

    def first_step(k, _):
        for_partner(k)
        return 0

    def both_step(k, _):
        for_partner(k + 2)
        for_chip(k)
        return 0

    def last_step(k, _):
        for_chip(k)
        return 0

    lax.fori_loop(0, 2, first_step, 0)
    lax.fori_loop(0, R - 2, both_step, 0)
    lax.fori_loop(R - 2, R - 1, last_step, 0)
    total = down(me)
    remote(
        send_a.at[R - 1], recv_a.at[R - 1], a_send.at[R - 1], a_recv.at[R - 1], row, other
    ).wait()
    own_sum[...] = total + recv_a[R - 1].astype(f32) + mid[...].astype(f32)

    def collect(k, _):
        source = target_of(lax.rem(k + R - 2, R - 1))
        remote(
            send_b.at[k], recv_b.at[source], b_send.at[k], b_recv.at[source], source, sec
        ).wait_recv()
        own_sum[...] += recv_b[source].astype(f32)
        return 0

    lax.fori_loop(0, R - 1, collect, 0)
    out[...] = own_sum[...].astype(jnp.bfloat16)

    def drain(k, _):
        remote(
            send_b.at[k], recv_b.at[row], b_send.at[k], b_recv.at[row], row, other
        ).wait_send()
        return 0

    lax.fori_loop(0, R - 1, drain, 0)
    for i in range(per):
        dest = to_group * per + i

        @pl.when(dest != me)
        def _():
            remote(
                bc_out, bc_all.at[slot], bc_send.at[i], bc_recv.at[slot], row, other
            ).wait_send()

    for copy in pending:
        copy.wait_send()
    gather_drain(hid_all, h_send, h_recv)
    gather_drain(mid_all, m_send, m_recv)
    store_ssm.wait()


def hand_over(*refs):
    count = (len(refs) - 2) // 3
    ins, outs, held = refs[:count], refs[count : 2 * count], refs[2 * count : 3 * count]
    in_sem, out_sem = refs[3 * count], refs[3 * count + 1]
    parts = []
    for i in range(count):
        cuts = 4 if i == 1 else 1
        size = ins[i].shape[0] // cuts
        for c in range(cuts):
            at = pl.ds(c * size, size)
            n = len(parts)
            parts.append(
                (
                    pltpu.make_async_copy(ins[i].at[at], held[i].at[at], in_sem.at[n]),
                    pltpu.make_async_copy(held[i].at[at], outs[i].at[at], out_sem.at[n]),
                )
            )
    for first, _ in parts:
        first.start()
    for first, second in parts:
        first.wait()
        second.start()
    for _, second in parts:
        second.wait()


def fused_body(
    hidden, norm_in_gain, zx_weight, bc_weight, dt_weight, dt_bias, decay_log, skip_gain,
    conv_x_weight, conv_x_bias, conv_bc_weight, conv_bc_bias, conv_x_state, conv_bc_state,
    ssm_state, gate_norm_weight, out_weight, norm_mid_gain, up_weight, down_weight, valid,
):
    R = lax.axis_size("row")
    N = 2 * R
    rows, wd = hidden.shape
    model = up_weight.shape[0]
    p = zx_weight.shape[3]
    cb = bc_weight.shape[1]
    ff = up_weight.shape[1]
    bf16, f32 = jnp.bfloat16, jnp.float32
    vm, hbm = pl.BlockSpec(memory_space=pltpu.VMEM), pl.BlockSpec(memory_space=pl.ANY)
    dma = pltpu.SemaphoreType.DMA
    operands = (
        hidden,
        norm_in_gain.reshape(1, model),
        jnp.transpose(zx_weight, (1, 2, 3, 0)).reshape(2 * p, model),
        bc_weight,
        dt_weight.reshape(1, model),
        dt_bias.reshape(1, 1),
        decay_log.reshape(1, 1),
        skip_gain.reshape(1, 1),
        conv_x_weight.reshape(4, p),
        conv_x_bias.reshape(1, p),
        conv_bc_weight,
        conv_bc_bias.reshape(1, cb),
        jnp.transpose(conv_x_state, (1, 2, 0, 3)).reshape(3, rows, p),
        jnp.transpose(conv_bc_state, (1, 0, 2)),
        ssm_state.reshape(rows, p, STATE),
        gate_norm_weight.reshape(1, p),
        out_weight.reshape(p, model),
        norm_mid_gain.reshape(1, model),
        up_weight,
        down_weight,
        valid.reshape(1, rows),
    )
    results = pl.pallas_call(
        functools.partial(staged_kernel, R),
        out_shape=(
            jax.ShapeDtypeStruct((rows, wd), bf16),
            jax.ShapeDtypeStruct((rows, p, STATE), bf16),
            jax.ShapeDtypeStruct((3, rows, p), bf16),
            jax.ShapeDtypeStruct((3, rows, cb), bf16),
        ),
        in_specs=[hbm] * 21,
        out_specs=(vm, hbm, vm, vm),
        scratch_shapes=[
            pltpu.VMEM((2 * p, model), bf16),
            pltpu.VMEM((model, cb), bf16),
            pltpu.VMEM((rows, p, STATE), bf16),
            pltpu.VMEM((model, ff), bf16),
            pltpu.VMEM((ff, model), bf16),
            pltpu.VMEM((N, rows, wd), bf16),
            pltpu.VMEM((N, p, wd), bf16),
            pltpu.VMEM((rows, cb), f32),
            pltpu.VMEM((2 * STATE // cb, rows, cb), f32),
            pltpu.VMEM((p, 128), f32),
            pltpu.VMEM((4, p, 128), f32),
            pltpu.VMEM((rows, wd), bf16),
            pltpu.VMEM((N, rows, wd), bf16),
            pltpu.VMEM((R // 2, rows, wd), bf16),
            pltpu.VMEM((R // 2, rows, wd), bf16),
            pltpu.VMEM((rows, ff), f32),
            pltpu.VMEM((R, rows, wd), bf16),
            pltpu.VMEM((R, rows, wd), bf16),
            pltpu.VMEM((R, rows, wd), bf16),
            pltpu.VMEM((R, rows, wd), bf16),
            pltpu.VMEM((rows, wd), f32),
            dma((6 + R // 2,)), dma((N,)), dma((N,)), dma((N,)), dma((N,)),
            dma((N // GROUPS,)), dma((2 * STATE // cb,)),
            dma((N,)), dma((N,)), dma((N,)), dma((N,)),
            dma((R,)), dma((R,)), dma((R,)), dma((R,)), dma((R,)), dma((R,)),
        ]
        + [pltpu.VMEM(operands[i].shape, operands[i].dtype) for i in SMALL]
        + [dma((len(SMALL),))],
        compiler_params=pltpu.CompilerParams(
            collective_id=0, has_side_effects=True, vmem_limit_bytes=60 * 1024 * 1024
        ),
    )(*operands)
    out, new_ssm, new_cx, new_cb = pl.pallas_call(
        hand_over,
        out_shape=tuple(jax.ShapeDtypeStruct(v.shape, v.dtype) for v in results),
        in_specs=[hbm] * 4,
        out_specs=(hbm,) * 4,
        scratch_shapes=[pltpu.VMEM(v.shape, v.dtype) for v in results] + [dma((7,)), dma((7,))],
    )(*results)
    return (
        out,
        new_ssm.reshape(rows, 1, p, STATE),
        jnp.transpose(new_cx, (1, 0, 2)).reshape(rows, 3, 1, p),
        jnp.transpose(new_cb, (1, 0, 2)),
    )


def solution(mesh):
    chosen = fused_body if fits(mesh) else body
    return jax.shard_map(
        chosen,
        mesh=mesh,
        in_specs=(
            P("groups", ("row", "section")),
            P(),
            P(None, None, "row", "section"),
            P(None, ("row", "section")),
            P(None, "row"),
            P("row"),
            P("row"),
            P("row"),
            P(None, "row", "section"),
            P("row", "section"),
            P(None, ("row", "section")),
            P(("row", "section")),
            P("groups", None, "row", "section"),
            P("groups", None, ("row", "section")),
            P("groups", "row", "section", None),
            P("row", "section"),
            P("row", "section", None),
            P(),
            P(None, ("row", "section")),
            P(("row", "section"), None),
            P("groups"),
        ),
        out_specs=(
            P("groups", ("row", "section")),
            P("groups", "row", "section", None),
            P("groups", None, "row", "section"),
            P("groups", None, ("row", "section")),
        ),
        check_vma=False,
    )
```

```python
import functools

import jax
import jax.numpy as jnp
from jax import lax
from jax.experimental import pallas as pl
from jax.experimental.pallas import tpu as pltpu
from jax.sharding import PartitionSpec as P

D = 8192
HEAD_DIM = 64
STATE = 256
GROUPS = 4


def mean_norm(values, gain):
    return values * lax.rsqrt(jnp.mean(values * values, axis=-1, keepdims=True) + 1e-05) * gain


def body(
    hidden,
    norm_in_gain,
    zx_weight,
    bc_weight,
    dt_weight,
    dt_bias,
    decay_log,
    skip_gain,
    conv_x_weight,
    conv_x_bias,
    conv_bc_weight,
    conv_bc_bias,
    conv_x_state,
    conv_bc_state,
    ssm_state,
    gate_norm_weight,
    out_weight,
    norm_mid_gain,
    up_weight,
    down_weight,
    valid,
):
    row_count = hidden.shape[0]
    local_p = zx_weight.shape[3]
    full_rows = lax.all_gather(hidden, ("row", "section"), axis=1, tiled=True)
    normed = mean_norm(full_rows.astype(jnp.float32), norm_in_gain).astype(jnp.bfloat16)
    gate_inner = jnp.dot(
        normed, zx_weight.reshape(D, 2 * local_p), preferred_element_type=jnp.float32
    ).reshape(row_count, 2, 1, local_p)
    gate_part = gate_inner[:, 0]
    inner_pre = gate_inner[:, 1].astype(jnp.bfloat16)
    bc_pre = jnp.dot(normed, bc_weight, preferred_element_type=jnp.float32).astype(jnp.bfloat16)
    dt_raw = jnp.dot(normed, dt_weight, preferred_element_type=jnp.float32)
    taps_x = jnp.concatenate([conv_x_state, inner_pre[:, None]], axis=1)
    inner = jax.nn.silu(
        jnp.sum(taps_x.astype(jnp.float32) * conv_x_weight[None], axis=1) + conv_x_bias
    )
    taps_bc = jnp.concatenate([conv_bc_state, bc_pre[:, None]], axis=1)
    mixed_bc = jax.nn.silu(
        jnp.sum(taps_bc.astype(jnp.float32) * conv_bc_weight[None], axis=1) + conv_bc_bias
    )
    all_bc = lax.all_gather(mixed_bc, ("row", "section"), axis=1, tiled=True)
    per_group = lax.axis_size("row") // GROUPS
    group_index = lax.axis_index("row") // per_group
    state_in = all_bc[:, : GROUPS * STATE].reshape(row_count, GROUPS, STATE)
    state_out = all_bc[:, GROUPS * STATE :].reshape(row_count, GROUPS, STATE)
    in_mine = lax.dynamic_slice_in_dim(state_in, group_index, 1, axis=1)
    out_mine = lax.dynamic_slice_in_dim(state_out, group_index, 1, axis=1)
    step_size = jax.nn.softplus(dt_raw + dt_bias[None])
    decay_rate = jnp.exp(-step_size * jnp.exp(decay_log)[None])
    previous = ssm_state.astype(jnp.float32)
    updated = (
        decay_rate[:, :, None, None] * previous
        + (step_size[:, :, None] * inner)[..., None] * in_mine[:, :, None, :]
    )
    readout = (
        jnp.einsum("rhpn,rhn->rhp", updated, out_mine, precision=lax.Precision.HIGHEST)
        + skip_gain[None, :, None] * inner
    )
    gated = readout * jax.nn.silu(gate_part)
    local_squares = jnp.sum(gated * gated, axis=(1, 2))
    group_pick = (jnp.arange(GROUPS) == group_index).astype(jnp.float32)
    group_sums = lax.psum(local_squares[:, None] * group_pick[None], ("row", "section"))
    group_size = per_group * HEAD_DIM
    group_mean = jnp.sum(group_sums * group_pick[None], axis=1) / group_size
    scaled = (gated * lax.rsqrt(group_mean + 1e-05)[:, None, None] * gate_norm_weight[None]).astype(
        jnp.bfloat16
    )
    mixer_terms = jnp.dot(
        scaled.reshape(row_count, local_p),
        out_weight.reshape(local_p, D),
        preferred_element_type=jnp.float32,
    )
    mixer_share = lax.psum_scatter(mixer_terms, ("row", "section"), scatter_dimension=1, tiled=True)
    middle = (hidden.astype(jnp.float32) + mixer_share).astype(jnp.bfloat16)
    middle_full = lax.all_gather(middle, ("row", "section"), axis=1, tiled=True)
    mlp_in = mean_norm(middle_full.astype(jnp.float32), norm_mid_gain).astype(jnp.bfloat16)
    up_values = jnp.dot(mlp_in, up_weight, preferred_element_type=jnp.float32)
    activated = jnp.square(jax.nn.relu(up_values)).astype(jnp.bfloat16)
    down_terms = jnp.dot(activated, down_weight, preferred_element_type=jnp.float32)
    down_share = lax.psum_scatter(down_terms, ("row", "section"), scatter_dimension=1, tiled=True)
    block_out = (middle.astype(jnp.float32) + down_share).astype(jnp.bfloat16)
    kept_rows = valid != 0
    new_ssm_state = jnp.where(kept_rows[:, None, None, None], updated, previous).astype(
        jnp.bfloat16
    )
    new_conv_x_state = jnp.where(kept_rows[:, None, None, None], taps_x[:, 1:], conv_x_state)
    new_conv_bc_state = jnp.where(kept_rows[:, None, None], taps_bc[:, 1:], conv_bc_state)
    return (block_out, new_ssm_state, new_conv_x_state, new_conv_bc_state)


HI = lax.Precision.HIGHEST
MESH = pl.DeviceIdType.MESH
NT = (((1,), (1,)), ((), ()))


def fits(mesh):
    return mesh.shape["section"] == 2 and mesh.shape["row"] == 2 * GROUPS


def silu(values):
    return values / (1.0 + jnp.exp(-values))


SMALL = (0, 1, 4, 5, 6, 7, 8, 9, 10, 11, 12, 13, 15, 17, 20)


def staged_kernel(R, *refs):
    count = len(SMALL)
    ins, rest, held, sem = list(refs[:21]), refs[21 : -count - 1], refs[-count - 1 : -1], refs[-1]
    copies = [pltpu.make_async_copy(ins[i], held[n], sem.at[n]) for n, i in enumerate(SMALL)]
    hid_source = ins[0]
    for n, i in enumerate(SMALL):
        ins[i] = held[n]
    fused_kernel(R, copies, hid_source, *ins, *rest)


def fused_kernel(
    R, small_copies, hid_source,
    hid, gin, zxt, bcw, dtt, dtb, dlog, skip, cxw, cxb, cbw, cbb, cxs, cbs, ssm, gnw, outw, gmid,
    upw, dnw, valid,
    out, new_ssm, new_cx, new_cb,
    zx_v, bc_v, ssm_v, up_v, dn_v, hid_all, owt, bc_out, bc_all, g_out, g_all, mid, mid_all,
    send_m, recv_m, act, send_a, recv_a, send_b, recv_b, own_sum,
    w_sem, h_send, h_recv, o_send, o_recv, bc_send, bc_recv, g_send, g_recv, m_send, m_recv,
    a_send, a_recv, b_send, b_recv, x_send, x_recv,
):
    N = 2 * R
    grp, row, sec = lax.axis_index("groups"), lax.axis_index("row"), lax.axis_index("section")
    me = row * 2 + sec
    other = 1 - sec
    rows, wd = hid.shape
    local_p = zxt.shape[0] // 2
    model = upw.shape[0]

    def remote(src, dst, ssem, rsem, r, s):
        return pltpu.make_async_remote_copy(
            src_ref=src, dst_ref=dst, send_sem=ssem, recv_sem=rsem,
            device_id=(grp, r, s), device_id_type=MESH,
        )

    pending = []

    loads = [
        pltpu.make_async_copy(bcw, bc_v, w_sem.at[0]),
        pltpu.make_async_copy(zxt, zx_v, w_sem.at[1]),
        pltpu.make_async_copy(ssm, ssm_v, w_sem.at[2]),
        pltpu.make_async_copy(upw, up_v, w_sem.at[3]),
        pltpu.make_async_copy(dnw, dn_v, w_sem.at[4]),
    ]

    barrier = pltpu.get_barrier_semaphore()
    for k in range(1, N):
        peer = lax.rem(me + k, N)
        pl.semaphore_signal(
            barrier, inc=1, device_id=(grp, peer // 2, peer % 2), device_id_type=MESH
        )
    for copy in small_copies + loads:
        copy.start()
    pl.semaphore_wait(barrier, N - 1)

    Z = R // 2
    z, x = row // 2, row % 2

    def gather_start(src, buf, ssem, rsem):
        for k in range(1, Z):
            remote(
                src, buf.at[me], ssem.at[k], rsem.at[me], lax.rem(z + k, Z) * 2 + x, sec
            ).start()
        remote(src, buf.at[me], ssem.at[0], rsem.at[me], z * 2 + 1 - x, sec).start()
        remote(src, buf.at[me], ssem.at[Z], rsem.at[me], row, other).start()

    visits = tuple(range(16))

    def gather_step(i, buf, ssem, rsem):
        j = jnp.int32(0)
        for position, visit in enumerate(visits):
            j = jnp.where(i == position, visit, j)
        k, far, cross = j % Z, (j // Z) % 2, j // (2 * Z)
        blk = (lax.rem(z + k, Z) * 2 + lax.rem(x + far, 2)) * 2 + lax.rem(sec + cross, 2)
        block = buf.at[blk]

        @pl.when(j > 0)
        def _():
            remote(block, block, ssem.at[0], rsem.at[blk], row, other).wait_recv()

        @pl.when(jnp.logical_and(j > 0, j < Z))
        def _():
            remote(
                block, block, ssem.at[Z + j], rsem.at[blk], z * 2 + 1 - x, sec
            ).start()

        @pl.when(jnp.logical_and(j > 0, j < 2 * Z))
        def _():
            remote(block, block, ssem.at[2 * Z + j - 1], rsem.at[blk], row, other).start()

        return blk

    def gather_drain(buf, ssem, rsem):
        def step(i, _):
            remote(buf.at[me], buf.at[me], ssem.at[i], rsem.at[me], row, other).wait_send()
            return 0

        lax.fori_loop(0, 4 * Z - 1, step, 0)

    gather_start(hid_source, hid_all, h_send, h_recv)
    for copy in small_copies:
        copy.wait()
    hid_all[me] = hid[...]

    eye = (
        lax.broadcasted_iota(jnp.int32, (local_p, local_p), 0)
        == lax.broadcasted_iota(jnp.int32, (local_p, local_p), 1)
    ).astype(jnp.float32)

    def turn(values):
        return lax.dot_general(eye, values, NT, precision=HI, preferred_element_type=jnp.float32)

    f32 = jnp.float32
    valid_row = (valid[...] != 0).astype(f32)
    valid_col = turn(valid_row)
    pre_x = cxb[...] + sum(cxs[t].astype(f32) * cxw[t : t + 1, :] for t in range(3))
    pre_x_t = turn(pre_x)
    tap_t = turn(cxw[3:4, :])
    gnw_t = turn(gnw[...])
    pre_bc = cbb[...] + sum(cbs[t].astype(f32) * cbw[t : t + 1, :] for t in range(3))

    def add_squares(total, values):
        squares = values * values
        return total + sum(squares[:, i : i + 128] for i in range(0, wd, 128))

    def inverse(total):
        return lax.rsqrt(jnp.sum(total, axis=1, keepdims=True) / model + 1e-05)

    loads[0].wait()
    loads[1].wait()

    def project(j, carry):
        total, acc_bc, acc_zx, acc_dt = carry
        b = gather_step(j, hid_all, h_send, h_recv)
        at = pl.ds(pl.multiple_of(b * wd, wd), wd)
        values = hid_all[b].astype(f32)
        total = add_squares(total, values)
        fed = (values * gin[:, at]).astype(jnp.bfloat16)
        acc_bc += jnp.dot(fed, bc_v[at, :], preferred_element_type=f32)
        acc_zx += lax.dot_general(zx_v[:, at], fed, NT, preferred_element_type=f32)
        dt_rows = jnp.broadcast_to(dtt[:, at].astype(f32), (16, wd)).astype(jnp.bfloat16)
        acc_dt += lax.dot_general(dt_rows, fed, NT, preferred_element_type=f32)
        return total, acc_bc, acc_zx, acc_dt

    total, acc_bc, acc_zx, acc_dt = lax.fori_loop(
        0, N, project,
        (
            jnp.zeros((rows, 128), f32),
            jnp.zeros((rows, bc_v.shape[1]), f32),
            jnp.zeros((2 * local_p, rows), f32),
            jnp.zeros((16, rows), f32),
        ),
    )
    scale = inverse(total)
    eye_rows = (
        lax.broadcasted_iota(jnp.int32, (rows, rows), 0)
        == lax.broadcasted_iota(jnp.int32, (rows, rows), 1)
    ).astype(f32)
    scale_row = jnp.sum(eye_rows * scale, axis=0, keepdims=True)
    acc_bc, acc_zx, acc_dt = acc_bc * scale, acc_zx * scale_row, acc_dt * scale_row
    bc_pre = acc_bc.astype(jnp.bfloat16).astype(f32)
    mixed_bc = silu(pre_bc + bc_pre * cbw[3:4, :])
    bc_out[...] = mixed_bc

    cb = bc_v.shape[1]
    parts = STATE // cb
    half = me // (N // 2)
    to_group = lax.rem(me, N // 2) // parts
    slot = half * parts + lax.rem(me, parts)
    per = N // GROUPS
    my_group = me // per
    for i in range(per):
        dest = to_group * per + i

        @pl.when(dest != me)
        def _():
            remote(
                bc_out, bc_all.at[slot], bc_send.at[i], bc_recv.at[slot], dest // 2, dest % 2
            ).start()

        @pl.when(dest == me)
        def _():
            bc_all[slot] = bc_out[...]

    place = x * 2 + sec
    spots = [(1 - x, sec), (row % 2, other), (1 - x, other)]
    for i, (px, pc) in enumerate(spots):
        for t in range(Z):
            at = pl.ds(pl.multiple_of((t * 4 + px * 2 + pc) * wd, wd), wd)
            copy = remote(
                outw.at[:, at], owt.at[t * 4 + place], o_send.at[i * Z + t],
                o_recv.at[t * 4 + place], z * 2 + px, pc,
            )
            copy.start()
            pending.append(copy)
    own_w = []
    for t in range(Z):
        at = pl.ds(pl.multiple_of((t * 4 + place) * wd, wd), wd)
        own_w.append(
            pltpu.make_async_copy(outw.at[:, at], owt.at[t * 4 + place], w_sem.at[6 + t])
        )
        own_w[-1].start()

    gate_t = silu(acc_zx[:local_p])
    inner_pre_t = acc_zx[local_p:].astype(jnp.bfloat16).astype(f32)
    inner_t = silu(pre_x_t + inner_pre_t * tap_t)
    dt_sum = acc_dt[0:1] + dtb[...]
    step_size = jnp.maximum(dt_sum, 0.0) + jnp.log1p(jnp.exp(-jnp.abs(dt_sum)))
    decay = jnp.exp(-step_size * jnp.exp(dlog[...]))
    driven_t = inner_t * step_size
    keep_x = jnp.broadcast_to(valid_col, (rows, local_p)) > 0.5
    keep_bc = jnp.broadcast_to(valid_col, (rows, cb)) > 0.5
    last_x = turn(inner_pre_t)
    for t in range(3):
        later_x = last_x if t == 2 else cxs[t + 1].astype(f32)
        later_bc = bc_pre if t == 2 else cbs[t + 1].astype(f32)
        new_cx[t] = jnp.where(keep_x, later_x, cxs[t].astype(f32)).astype(jnp.bfloat16)
        new_cb[t] = jnp.where(keep_bc, later_bc, cbs[t].astype(f32)).astype(jnp.bfloat16)
    loads[2].wait()

    for h in range(2):
        for p in range(parts):
            source = h * (N // 2) + my_group * parts + p

            @pl.when(source != me)
            def _():
                remote(
                    bc_out, bc_all.at[h * parts + p], bc_send.at[0], bc_recv.at[h * parts + p],
                    row, other,
                ).wait_recv()

    state_in = jnp.concatenate([bc_all[p] for p in range(parts)], axis=1)
    state_out = jnp.concatenate([bc_all[parts + p] for p in range(parts)], axis=1)

    lane = lax.broadcasted_iota(jnp.int32, (local_p, rows), 1)

    def updated(r):
        previous = ssm_v[r].astype(f32)
        value = decay[0:1, r : r + 1] * previous + driven_t[:, r : r + 1] * state_in[r : r + 1, :]
        return previous, value

    read_t = jnp.zeros((local_p, rows), f32)
    for r in range(rows):
        _, value = updated(r)
        column = jnp.sum(value * state_out[r : r + 1, :], axis=1, keepdims=True)
        read_t = jnp.where(lane == r, column, read_t)
    gated_t = (read_t + skip[...] * inner_t) * gate_t
    g_out[:, 0:rows] = gated_t
    g_out[:, rows : rows + 1] = gnw_t
    for i, (px, pc) in enumerate(spots):
        copy = remote(
            g_out, g_all.at[place], g_send.at[i], g_recv.at[place], z * 2 + px, pc
        )
        copy.start()
        pending.append(copy)
    g_all[place] = g_out[...]

    for r in range(rows):
        previous, value = updated(r)
        keep = jnp.broadcast_to(valid_row[0:1, r : r + 1], value.shape) > 0.5
        ssm_v[r] = jnp.where(keep, value, previous).astype(jnp.bfloat16)
    store_ssm = pltpu.make_async_copy(ssm_v, new_ssm, w_sem.at[5])
    store_ssm.start()

    for copy in own_w:
        copy.wait()
    for px, pc in spots:
        there = px * 2 + pc
        for t in range(Z):
            spot = t * 4 + there
            remote(
                owt.at[spot], owt.at[spot], o_send.at[0], o_recv.at[spot], row, other
            ).wait_recv()
    for px, pc in spots:
        there = px * 2 + pc
        remote(
            g_all.at[there], g_all.at[there], g_send.at[0], g_recv.at[there], row, other
        ).wait_recv()

    pieces = [g_all[i, :, 0:rows] for i in range(4)]
    squares = sum(jnp.sum(piece * piece, axis=0, keepdims=True) for piece in pieces)
    norm = lax.rsqrt(squares / (4 * local_p) + 1e-05)
    scaled_t = jnp.concatenate(
        [pieces[i] * norm * g_all[i, :, rows : rows + 1] for i in range(4)], axis=0
    ).astype(jnp.bfloat16)
    scaled = lax.dot_general(
        eye_rows.astype(jnp.bfloat16), scaled_t, NT, preferred_element_type=f32
    ).astype(jnp.bfloat16)

    def mixer(t):
        weights = owt[pl.ds(t * 4, 4)].reshape(4 * local_p, wd)
        return jnp.dot(scaled, weights, preferred_element_type=f32)

    for k in (2, 1, 3):
        t = lax.rem(z + k, Z)
        send_m[k] = mixer(t).astype(jnp.bfloat16)
        copy = remote(
            send_m.at[k], recv_m.at[z], x_send.at[k], x_recv.at[z], t * 2 + x, sec
        )
        copy.start()
        pending.append(copy)
    mixed = hid[...].astype(f32) + mixer(z)
    for k in (1, 3, 2):
        t = lax.rem(z + k, Z)
        remote(
            recv_m.at[t], recv_m.at[t], x_send.at[0], x_recv.at[t], row, other
        ).wait_recv()
        mixed += recv_m[t].astype(f32)
    mid[...] = mixed.astype(jnp.bfloat16)
    gather_start(mid, mid_all, m_send, m_recv)
    mid_all[me] = mid[...]
    loads[3].wait()
    act[...] = jnp.zeros_like(act)

    def up_step(j, total):
        b = gather_step(j, mid_all, m_send, m_recv)
        at = pl.ds(pl.multiple_of(b * wd, wd), wd)
        values = mid_all[b].astype(f32)
        fed = (values * gmid[:, at]).astype(jnp.bfloat16)
        act[...] += jnp.dot(fed, up_v[at, :], preferred_element_type=f32)
        return add_squares(total, values)

    total = lax.fori_loop(0, N, up_step, jnp.zeros((rows, 128), f32))
    activated = jnp.square(jnp.maximum(act[...] * inverse(total), 0.0)).astype(jnp.bfloat16)
    loads[4].wait()

    def down(block):
        at = pl.ds(pl.multiple_of(block * wd, wd), wd)
        return jnp.dot(activated, dn_v[:, at], preferred_element_type=f32)

    def target_of(k):
        hop = jnp.where(k < 2, 2, jnp.where(k < 4, 1, jnp.where(k < 6, 3, 0)))
        return lax.rem(z + hop, Z) * 2 + lax.rem(x + 1 + k, 2)

    def for_partner(k):
        send_a[k] = down(target_of(k) * 2 + other).astype(jnp.bfloat16)
        remote(send_a.at[k], recv_a.at[k], a_send.at[k], a_recv.at[k], row, other).start()

    def for_chip(k):
        target = target_of(k)
        part = down(target * 2 + sec)
        remote(send_a.at[k], recv_a.at[k], a_send.at[k], a_recv.at[k], row, other).wait()
        send_b[k] = (part + recv_a[k].astype(f32)).astype(jnp.bfloat16)
        remote(send_b.at[k], recv_b.at[row], b_send.at[k], b_recv.at[row], target, sec).start()

    def first_step(k, _):
        for_partner(k)
        return 0

    def both_step(k, _):
        for_partner(k + 2)
        for_chip(k)
        return 0

    def last_step(k, _):
        for_chip(k)
        return 0

    lax.fori_loop(0, 2, first_step, 0)
    lax.fori_loop(0, R - 2, both_step, 0)
    lax.fori_loop(R - 2, R - 1, last_step, 0)
    total = down(me)
    remote(
        send_a.at[R - 1], recv_a.at[R - 1], a_send.at[R - 1], a_recv.at[R - 1], row, other
    ).wait()
    own_sum[...] = total + recv_a[R - 1].astype(f32) + mid[...].astype(f32)

    def collect(k, _):
        source = target_of(lax.rem(k + R - 2, R - 1))
        remote(
            send_b.at[k], recv_b.at[source], b_send.at[k], b_recv.at[source], source, sec
        ).wait_recv()
        own_sum[...] += recv_b[source].astype(f32)
        return 0

    lax.fori_loop(0, R - 1, collect, 0)
    out[...] = own_sum[...].astype(jnp.bfloat16)

    def drain(k, _):
        remote(
            send_b.at[k], recv_b.at[row], b_send.at[k], b_recv.at[row], row, other
        ).wait_send()
        return 0

    lax.fori_loop(0, R - 1, drain, 0)
    for i in range(per):
        dest = to_group * per + i

        @pl.when(dest != me)
        def _():
            remote(
                bc_out, bc_all.at[slot], bc_send.at[i], bc_recv.at[slot], row, other
            ).wait_send()

    for copy in pending:
        copy.wait_send()
    gather_drain(hid_all, h_send, h_recv)
    gather_drain(mid_all, m_send, m_recv)
    store_ssm.wait()


def hand_over(*refs):
    count = (len(refs) - 2) // 3
    ins, outs, held = refs[:count], refs[count : 2 * count], refs[2 * count : 3 * count]
    in_sem, out_sem = refs[3 * count], refs[3 * count + 1]
    parts = []
    for i in range(count):
        cuts = 4 if i == 1 else 1
        size = ins[i].shape[0] // cuts
        for c in range(cuts):
            at = pl.ds(c * size, size)
            n = len(parts)
            parts.append(
                (
                    pltpu.make_async_copy(ins[i].at[at], held[i].at[at], in_sem.at[n]),
                    pltpu.make_async_copy(held[i].at[at], outs[i].at[at], out_sem.at[n]),
                )
            )
    for first, _ in parts:
        first.start()
    for first, second in parts:
        first.wait()
        second.start()
    for _, second in parts:
        second.wait()


def fused_body(
    hidden, norm_in_gain, zx_weight, bc_weight, dt_weight, dt_bias, decay_log, skip_gain,
    conv_x_weight, conv_x_bias, conv_bc_weight, conv_bc_bias, conv_x_state, conv_bc_state,
    ssm_state, gate_norm_weight, out_weight, norm_mid_gain, up_weight, down_weight, valid,
):
    R = lax.axis_size("row")
    N = 2 * R
    rows, wd = hidden.shape
    model = up_weight.shape[0]
    p = zx_weight.shape[3]
    cb = bc_weight.shape[1]
    ff = up_weight.shape[1]
    bf16, f32 = jnp.bfloat16, jnp.float32
    vm, hbm = pl.BlockSpec(memory_space=pltpu.VMEM), pl.BlockSpec(memory_space=pl.ANY)
    dma = pltpu.SemaphoreType.DMA
    operands = (
        hidden,
        norm_in_gain.reshape(1, model),
        jnp.transpose(zx_weight, (1, 2, 3, 0)).reshape(2 * p, model),
        bc_weight,
        dt_weight.reshape(1, model),
        dt_bias.reshape(1, 1),
        decay_log.reshape(1, 1),
        skip_gain.reshape(1, 1),
        conv_x_weight.reshape(4, p),
        conv_x_bias.reshape(1, p),
        conv_bc_weight,
        conv_bc_bias.reshape(1, cb),
        jnp.transpose(conv_x_state, (1, 2, 0, 3)).reshape(3, rows, p),
        jnp.transpose(conv_bc_state, (1, 0, 2)),
        ssm_state.reshape(rows, p, STATE),
        gate_norm_weight.reshape(1, p),
        out_weight.reshape(p, model),
        norm_mid_gain.reshape(1, model),
        up_weight,
        down_weight,
        valid.reshape(1, rows),
    )
    results = pl.pallas_call(
        functools.partial(staged_kernel, R),
        out_shape=(
            jax.ShapeDtypeStruct((rows, wd), bf16),
            jax.ShapeDtypeStruct((rows, p, STATE), bf16),
            jax.ShapeDtypeStruct((3, rows, p), bf16),
            jax.ShapeDtypeStruct((3, rows, cb), bf16),
        ),
        in_specs=[hbm] * 21,
        out_specs=(vm, hbm, vm, vm),
        scratch_shapes=[
            pltpu.VMEM((2 * p, model), bf16),
            pltpu.VMEM((model, cb), bf16),
            pltpu.VMEM((rows, p, STATE), bf16),
            pltpu.VMEM((model, ff), bf16),
            pltpu.VMEM((ff, model), bf16),
            pltpu.VMEM((N, rows, wd), bf16),
            pltpu.VMEM((N, p, wd), bf16),
            pltpu.VMEM((rows, cb), f32),
            pltpu.VMEM((2 * STATE // cb, rows, cb), f32),
            pltpu.VMEM((p, 128), f32),
            pltpu.VMEM((4, p, 128), f32),
            pltpu.VMEM((rows, wd), bf16),
            pltpu.VMEM((N, rows, wd), bf16),
            pltpu.VMEM((R // 2, rows, wd), bf16),
            pltpu.VMEM((R // 2, rows, wd), bf16),
            pltpu.VMEM((rows, ff), f32),
            pltpu.VMEM((R, rows, wd), bf16),
            pltpu.VMEM((R, rows, wd), bf16),
            pltpu.VMEM((R, rows, wd), bf16),
            pltpu.VMEM((R, rows, wd), bf16),
            pltpu.VMEM((rows, wd), f32),
            dma((6 + R // 2,)), dma((N,)), dma((N,)), dma((N,)), dma((N,)),
            dma((N // GROUPS,)), dma((2 * STATE // cb,)),
            dma((N,)), dma((N,)), dma((N,)), dma((N,)),
            dma((R,)), dma((R,)), dma((R,)), dma((R,)), dma((R,)), dma((R,)),
        ]
        + [pltpu.VMEM(operands[i].shape, operands[i].dtype) for i in SMALL]
        + [dma((len(SMALL),))],
        compiler_params=pltpu.CompilerParams(
            collective_id=0, has_side_effects=True, vmem_limit_bytes=60 * 1024 * 1024
        ),
    )(*operands)
    out, new_ssm, new_cx, new_cb = pl.pallas_call(
        hand_over,
        out_shape=tuple(jax.ShapeDtypeStruct(v.shape, v.dtype) for v in results),
        in_specs=[hbm] * 4,
        out_specs=(hbm,) * 4,
        scratch_shapes=[pltpu.VMEM(v.shape, v.dtype) for v in results] + [dma((7,)), dma((7,))],
    )(*results)
    return (
        out,
        new_ssm.reshape(rows, 1, p, STATE),
        jnp.transpose(new_cx, (1, 0, 2)).reshape(rows, 3, 1, p),
        jnp.transpose(new_cb, (1, 0, 2)),
    )


def solution(mesh):
    chosen = fused_body if fits(mesh) else body
    return jax.shard_map(
        chosen,
        mesh=mesh,
        in_specs=(
            P("groups", ("row", "section")),
            P(),
            P(None, None, "row", "section"),
            P(None, ("row", "section")),
            P(None, "row"),
            P("row"),
            P("row"),
            P("row"),
            P(None, "row", "section"),
            P("row", "section"),
            P(None, ("row", "section")),
            P(("row", "section")),
            P("groups", None, "row", "section"),
            P("groups", None, ("row", "section")),
            P("groups", "row", "section", None),
            P("row", "section"),
            P("row", "section", None),
            P(),
            P(None, ("row", "section")),
            P(("row", "section"), None),
            P("groups"),
        ),
        out_specs=(
            P("groups", ("row", "section")),
            P("groups", "row", "section", None),
            P("groups", None, "row", "section"),
            P("groups", None, ("row", "section")),
        ),
        check_vma=False,
    )
```
